512 devices in a mesh: pair: 16 (over x, y_lo), aux: 32 (over y_hi, z, core).
Axes of the slice: x: 4, y: 8 (y_hi: 2, y_lo: 4; y = y_hi * 4 + y_lo), z: 8, core: 2. Of those that a mesh axis runs over, the one named last changes fastest.
Arguments:
- amplitudes: bfloat16 [16, 512, 512], P('pair', 'aux'), may hold values from -6 to 6
- factors: bfloat16 [4096, 512, 512], P('aux', 'pair'), may hold values from -0.03125 to 0.03125
- hole_weights: float32 [16, 16], replicated, may hold values from -1.5 to 1.5
- driver: float32 [16, 6, 512], P('pair', None, 'aux'), may hold values from -6 to 6
- eps_vir: float32 [512], replicated, may hold values from 0.5 to 3
- pair_energy: float32 [16], P('pair'), may hold values from -3 to -0.5
Outputs:
- residual: float32 [16, 6, 512], P('pair', None, 'aux')
- new_amps: float32 [16, 6, 512], P('pair', None, 'aux')
The draws below stay inside these ranges and needn't reach their ends.
All inputs are finite; a program needn't handle non-finite values.
Results may differ from the reference program's by a relative error of at most 0.0003.
Values may be sent and summed in bfloat16 or wider, within the bound.
No kernel may reach another device: no remote copies, remote signals or barrier semaphores. Data moves between devices by JAX's collectives and lax.ppermute only.
A program may use at most 64 MiB of HBM per device.

```python
import jax
import jax.numpy as jnp
from jax import lax

V = 512
NAUX = 4096
A = 6
P_SIZE = 16


def block_levels(key, extent, pieces, least, largest):
    level, own = 1.0, jax.random.fold_in(key, 6)
    for axis_at, parts in pieces:
        draws = jnp.exp(jax.random.uniform(jax.random.fold_in(own, axis_at), (parts,), jnp.float32, least / len(pieces), largest / len(pieces)))
        level = level * jnp.repeat(draws, extent[axis_at] // parts).reshape([-1 if axis == axis_at else 1 for axis in range(len(extent))])
    return level


def scatter_about(own_key, dims, width, reach, cuts=(), dtype=jnp.bfloat16):
    gain = block_levels(own_key, dims, cuts, -0.22, 0.18) if cuts else 1.0
    entries = jax.random.normal(own_key, dims, jnp.float32) * width * gain
    return jnp.minimum(jnp.maximum(entries, -reach), reach).astype(dtype)


def setup_inputs(seed: int = 0) -> dict:
    key_of = jax.random.split(jax.random.key(seed), 7)
    return {
        "amplitudes": scatter_about(key_of[0], (P_SIZE, V, V), 1.0, 6.0, ((0, 16), (1, 32))),
        "factors": scatter_about(key_of[1], (NAUX, V, V), (V * 64) ** -0.5, 0.03125, ((0, 32), (1, 16))),
        "hole_weights": scatter_about(key_of[2], (P_SIZE, P_SIZE), P_SIZE ** -0.5, 1.5, (), jnp.float32),
        "driver": scatter_about(key_of[3], (P_SIZE, A, V), 1.0, 6.0, ((0, 16), (2, 32)), jnp.float32),
        "eps_vir": jnp.clip(jax.random.uniform(key_of[4], (V,), jnp.float32, 0.5, 3.0), 0.5, 3.0),
        "pair_energy": jnp.clip(-3.0 + 2.5 * jax.random.uniform(key_of[5], (P_SIZE,), jnp.float32) ** block_levels(key_of[5], (P_SIZE,), ((0, 16),), -0.2, 0.2), -3.0, -0.5),
    }


def reference(amplitudes, factors, hole_weights, driver, eps_vir, pair_energy):
    block_size = min(128, NAUX)
    block_count = NAUX // block_size
    amp_wide = amplitudes.astype(jnp.float32)
    stacked = factors.reshape(block_count, block_size, V, V)

    def add_block(total, factor_block):
        wide = factor_block.astype(jnp.float32)
        halves = jnp.einsum("qac,pcd->paqd", wide[:, :A, :], amp_wide, precision=lax.Precision.HIGHEST).astype(jnp.bfloat16)
        term = jnp.einsum("paqd,qbd->pab", halves.astype(jnp.float32), wide, precision=lax.Precision.HIGHEST)
        return total + term, None

    particle, unused = lax.scan(add_block, jnp.zeros((P_SIZE, A, V), jnp.float32), stacked)
    amp_window = amp_wide[:, :A, :]
    hole_term = jnp.einsum("pk,kab->pab", hole_weights, amp_window, precision=lax.Precision.HIGHEST)
    residual = driver + particle + hole_term
    denominator = eps_vir[:A][None, :, None] + eps_vir[None, None, :] - pair_energy[:, None, None]
    new_amps = amp_window - residual / denominator
    return residual, new_amps
```

```python
import jax
import jax.numpy as jnp
from jax import lax
from jax.experimental import pallas as pl
from jax.experimental.pallas import tpu as pltpu
from jax.sharding import Mesh
from jax.sharding import PartitionSpec as P

AXES = ("x", "ylo", "yhi", "z", "core")
PAIR = ("x", "ylo")
AUX = ("yhi", "z", "core")
Y = ("ylo", "yhi")
BF16 = jnp.bfloat16
F32 = jnp.float32
BLOCK_Q = 8


def shifted(array, axis, by):
    if axis == "x":
        count = lax.axis_size("x")
        return lax.ppermute(array, "x", [(i, (i + by) % count) for i in range(count)])
    lows, highs = lax.axis_size("ylo"), lax.axis_size("yhi")

    def index(y):
        return (y % lows) * highs + y // lows

    full = lows * highs
    return lax.ppermute(array, Y, [(index(y), index((y + by) % full)) for y in range(full)])


def ring(array, axis):
    behind, ahead = shifted(array, axis, 1), shifted(array, axis, -1)
    half = array.shape[0] // 2
    return behind, ahead, shifted(behind[:half], axis, 1), shifted(ahead[half:], axis, -1)


def swapped(array):
    return lax.ppermute(array, "core", [(0, 1), (1, 0)])


def window_of(factors, rows):
    parts = lax.axis_size("x")
    lows = lax.axis_size("ylo")
    wide = jnp.transpose(factors[:, :rows, :], (1, 0, 2))
    quarter = wide.shape[1] // parts
    pieces = [wide[:, i * quarter : (i + 1) * quarter, :] for i in range(parts)]
    x, ylo = lax.axis_index("x"), lax.axis_index("ylo")
    mine = jnp.where((x == 0) & (ylo == 0), pieces[0], jnp.zeros_like(pieces[0]))
    for i in range(1, parts):
        mine = mine + lax.ppermute(pieces[i], PAIR, [(0, i * lows)])
    spread = jnp.where(ylo == 0, mine, jnp.zeros_like(mine))
    for k in range(1, lows):
        spread = spread + lax.ppermute(mine, PAIR, [(i * lows, i * lows + k) for i in range(parts)])
    return lax.all_to_all(
        jnp.broadcast_to(spread[None], (parts, *spread.shape)), "x", 0, 0, tiled=True
    )


def ladder_kernel(scalars, f_own, f_other, w_own, w_other, *refs):
    amps, (out, head, halves) = refs[:-3], refs[-3:]
    rows = w_own.shape[1]
    per_piece = w_own.shape[2] // BLOCK_Q
    pieces = w_own.shape[0]
    blocks = pieces * per_piece
    depth = w_own.shape[3]
    columns = f_own.shape[2]
    span = rows * BLOCK_Q

    local = 0
    for chunk in amps:
        for k in range(chunk.shape[0]):
            amp = chunk[k]
            head[pl.ds(scalars[local], 1)] = amp[None, : head.shape[1], :]
            for which, w in enumerate((w_own, w_other)):
                for piece in range(pieces):
                    got = jnp.dot(
                        w[piece].reshape(rows * per_piece * BLOCK_Q, depth),
                        amp,
                        preferred_element_type=F32,
                    ).reshape(rows, per_piece, BLOCK_Q, columns)
                    for b in range(per_piece):
                        at = (which * blocks + piece * per_piece + b) * columns
                        halves[local * span : (local + 1) * span, at : at + columns] = (
                            got[:, b].reshape(span, columns).astype(BF16)
                        )
            local += 1
    total = None
    group = 8
    for which, f in enumerate((f_own, f_other)):
        for start in range(0, blocks, group):
            right = jnp.concatenate(
                [
                    f[(start + b) * BLOCK_Q : (start + b + 1) * BLOCK_Q].reshape(-1, columns)
                    for b in range(group)
                ],
                axis=1,
            )
            at = (which * blocks + start) * columns
            term = lax.dot_general(
                halves[:, at : at + group * columns],
                right,
                (((1,), (1,)), ((), ())),
                preferred_element_type=F32,
            )
            total = term if total is None else total + term
    width = f_own.shape[1]
    lanes = BLOCK_Q * width
    total = total.reshape(local * rows, BLOCK_Q, lanes)
    q = lax.broadcasted_iota(jnp.int32, total.shape, 1)
    lane = lax.broadcasted_iota(jnp.int32, total.shape, 2)
    folded = jnp.sum(jnp.where(lane // width == q, total, 0.0), axis=1)
    folded = folded[:, : lanes // 2] + folded[:, lanes // 2 :]
    folded = folded + pltpu.roll(folded, 64, 1)
    folded = folded + pltpu.roll(folded, 32, 1)
    for i in range(local):
        out[pl.ds(scalars[i], 1)] = folded[i * rows : (i + 1) * rows][None]


def per_device(amplitudes, factors, hole_weights, driver, eps_vir, pair_energy):
    pairs = hole_weights.shape[0]
    rows, columns = driver.shape[1], driver.shape[2]
    depth = factors.shape[2]
    half = depth // 2
    width = factors.shape[1]
    x, ylo, yhi, z, core = (lax.axis_index(name) for name in AXES)
    aux_index = lax.axis_index(AUX)
    pair_index = lax.axis_index(PAIR)
    xs, lows = lax.axis_size("x"), lax.axis_size("ylo")

    own = amplitudes[0]
    split = jnp.stack([own[:, :half], own[:, half:]])
    sent = jnp.tile(split[None], (lax.axis_size("yhi") * lax.axis_size("z"), 1, 1, 1))
    amp = lax.all_to_all(sent.reshape(-1, *split.shape[1:]), AUX, 0, 0, tiled=True)
    amp = amp.reshape(-1, half)

    f_other = swapped(lax.dynamic_slice_in_dim(factors, (1 - core) * half, half, 2))
    window = window_of(factors, rows)
    window_other = swapped(window)

    start = (aux_index * columns) % half
    here = lax.dynamic_slice_in_dim(amp[:rows], start, columns, 1)
    there = lax.dynamic_slice_in_dim(amp[:rows], (start + columns * (1 - 2 * core)) % half, columns, 1)
    amp_cols = jnp.where(core == yhi, here, swapped(there)).astype(F32)

    behind, ahead, first, last = ring(amp, "y")
    chunk = jnp.stack([amp, behind, ahead, jnp.concatenate([first, last])])
    amps = (chunk, *ring(chunk, "x"))
    offsets = (0, 1, -1, 2)
    places = [(i, k) for i in range(3) for k in range(4)] + [(3, k) for k in range(4)]
    order = jnp.stack(
        [((x - offsets[i]) % xs) * lows + (ylo - offsets[k]) % lows for i, k in places]
    ).astype(jnp.int32)
    scalars = jnp.concatenate([order, core[None].astype(jnp.int32)])

    head_rows = 16
    blocks = factors.shape[0] // BLOCK_Q
    span = rows * BLOCK_Q
    whole = pl.BlockSpec(memory_space=pltpu.VMEM)
    quarters = window.shape
    particle, head = pl.pallas_call(
        ladder_kernel,
        grid_spec=pltpu.PrefetchScalarGridSpec(
            num_scalar_prefetch=1,
            grid=(1,),
            in_specs=[
                pl.BlockSpec((factors.shape[0], width, half), lambda i, s: (0, 0, s[pairs])),
            ]
            + [whole] * (3 + len(amps)),
            out_specs=[whole, whole],
            scratch_shapes=[pltpu.VMEM((pairs * span, 2 * blocks * half), BF16)],
        ),
        out_shape=[
            jax.ShapeDtypeStruct((pairs, rows, 128), F32),
            jax.ShapeDtypeStruct((pairs, head_rows, half), BF16),
        ],
        compiler_params=pltpu.CompilerParams(vmem_limit_bytes=56 * 1024 * 1024),
        cost_estimate=pl.CostEstimate(
            flops=9_700_000_000, bytes_accessed=12_000_000, transcendentals=0
        ),
    )(scalars, factors, f_other, window, window_other, *amps)
    particle = particle[:, :, :width]

    place = (pair_index * width) % half
    near = lax.dynamic_slice_in_dim(head[:, :rows, :], place, width, 2).astype(F32)
    hole_term = jnp.einsum("pk,kab->pab", hole_weights, near, precision=lax.Precision.HIGHEST)
    chosen = (yhi == 0) & (z == 0) & (core == (pair_index * width) // half)
    partial_value = particle + jnp.where(chosen, hole_term, 0.0)

    tiles = partial_value.reshape(pairs, rows, width // columns, columns)
    tiles = jnp.transpose(tiles, (0, 2, 1, 3)).reshape(-1, 1, rows * columns)
    summed = jnp.sum(lax.all_to_all(tiles, AUX, 0, 0, tiled=True), axis=0)
    count = lax.axis_size(AUX)
    halves = width // columns
    moves = []
    for g in range(pairs):
        for j in range(count):
            moves.append((g * count + j, (j // halves) * count + halves * g + j % halves))
    summed = lax.ppermute(summed, AXES, moves).reshape(1, rows, columns)

    residual = driver + summed
    eps_cols = lax.dynamic_slice_in_dim(eps_vir, aux_index * columns, columns, 0)
    denominator = (
        eps_vir[:rows][None, :, None] + eps_cols[None, None, :] - pair_energy[:, None, None]
    )
    new_amps = amp_cols[None] - residual / denominator
    return (residual, new_amps)


def solution(mesh):
    finer = Mesh(mesh.devices.reshape(4, 4, 2, 8, 2), AXES)
    in_specs = (P(PAIR, AUX, None), P(AUX, PAIR, None), P(), P(PAIR, None, AUX), P(), P(PAIR))
    out_specs = (P(PAIR, None, AUX), P(PAIR, None, AUX))
    return jax.shard_map(
        per_device, mesh=finer, in_specs=in_specs, out_specs=out_specs, check_vma=False
    )
```

```python
import jax
import jax.numpy as jnp
from jax import lax
from jax.experimental import pallas as pl
from jax.experimental.pallas import tpu as pltpu
from jax.sharding import Mesh
from jax.sharding import PartitionSpec as P

AXES = ("x", "ylo", "yhi", "z", "core")
PAIR = ("x", "ylo")
AUX = ("yhi", "z", "core")
Y = ("ylo", "yhi")
BF16 = jnp.bfloat16
F32 = jnp.float32
BLOCK_Q = 8


def shifted(array, axis, by):
    if axis == "x":
        count = lax.axis_size("x")
        return lax.ppermute(array, "x", [(i, (i + by) % count) for i in range(count)])
    lows, highs = lax.axis_size("ylo"), lax.axis_size("yhi")

    def index(y):
        return (y % lows) * highs + y // lows

    full = lows * highs
    return lax.ppermute(array, Y, [(index(y), index((y + by) % full)) for y in range(full)])


def swapped(array):
    return lax.ppermute(array, "core", [(0, 1), (1, 0)])


def window_scattered(factors, rows):
    parts, lows = lax.axis_size("x"), lax.axis_size("ylo")
    wide = jnp.transpose(factors[:, :rows, :], (1, 0, 2))
    quarter = wide.shape[1] // parts
    pieces = [wide[:, i * quarter : (i + 1) * quarter, :] for i in range(parts)]
    first = (lax.axis_index("x") == 0) & (lax.axis_index("ylo") == 0)
    mine = jnp.where(first, pieces[0], jnp.zeros_like(pieces[0]))
    for i in range(1, parts):
        mine = mine + lax.ppermute(pieces[i], PAIR, [(0, i * lows)])
    return mine


def window_spread(mine):
    parts, lows = lax.axis_size("x"), lax.axis_size("ylo")
    spread = jnp.where(lax.axis_index("ylo") == 0, mine, jnp.zeros_like(mine))
    for k in range(1, lows):
        spread = spread + lax.ppermute(mine, PAIR, [(i * lows, i * lows + k) for i in range(parts)])
    return spread


def window_collected(quarter):
    parts = lax.axis_size("x")
    return lax.all_to_all(
        jnp.broadcast_to(quarter[None], (parts, *quarter.shape)), "x", 0, 0, tiled=True
    )


def half_sums(f_own, f_other, w_own, w_other, chunks, halves):
    pieces, rows, per_piece, depth = w_own.shape
    per_piece = per_piece // BLOCK_Q
    blocks = pieces * per_piece
    columns = f_own.shape[2]
    span = rows * BLOCK_Q
    count = 0
    for chunk in chunks:
        for k in range(chunk.shape[0]):
            amp = chunk[k]
            for which, w in enumerate((w_own, w_other)):
                got = jnp.dot(
                    w[...].reshape(blocks * span, depth), amp, preferred_element_type=F32
                ).reshape(pieces, rows, per_piece, BLOCK_Q, columns)
                for piece in range(pieces):
                    for b in range(per_piece):
                        at = (which * blocks + piece * per_piece + b) * columns
                        halves[count * span : (count + 1) * span, at : at + columns] = (
                            got[piece, :, b].reshape(span, columns).astype(BF16)
                        )
            count += 1
    total = None
    group = 8
    for which, f in enumerate((f_own, f_other)):
        for start in range(0, blocks, group):
            right = jnp.concatenate(
                [
                    f[(start + b) * BLOCK_Q : (start + b + 1) * BLOCK_Q].reshape(-1, columns)
                    for b in range(group)
                ],
                axis=1,
            )
            at = (which * blocks + start) * columns
            term = lax.dot_general(
                halves[:, at : at + group * columns],
                right,
                (((1,), (1,)), ((), ())),
                preferred_element_type=F32,
            )
            total = term if total is None else total + term
    width = f_own.shape[1]
    total = total.reshape(count * rows, BLOCK_Q, BLOCK_Q * width)
    q = lax.broadcasted_iota(jnp.int32, total.shape, 1)
    lane = lax.broadcasted_iota(jnp.int32, total.shape, 2)
    return jnp.sum(jnp.where(lane // width == q, total, 0.0), axis=1)


def early_kernel(scalars, f_own, f_other, w_own, w_other, *refs):
    chunks, (sums, heads, halves) = refs[:-3], refs[-3:]
    sums[...] = half_sums(f_own, f_other, w_own, w_other, chunks, halves)
    count = 0
    for chunk in chunks:
        for k in range(chunk.shape[0]):
            heads[count] = chunk[k, : heads.shape[1], :].astype(F32)
            count += 1


def late_kernel(chunk_count, scalars, f_own, f_other, w_own, w_other, hole_weights, *refs):
    chunks, refs = refs[:chunk_count], refs[chunk_count:]
    early, (out, halves, head, hole) = refs[:-4], refs[-4:]
    rows = w_own.shape[1]
    width = f_own.shape[1]
    pairs = hole_weights.shape[0]
    sums = [s[...] for s in early[0::2]]
    sums.append(half_sums(f_own, f_other, w_own, w_other, chunks, halves))
    sums = jnp.concatenate(sums, axis=0)

    local = 0
    for heads in early[1::2]:
        for k in range(heads.shape[0]):
            head[pl.ds(scalars[local], 1)] = heads[k][None]
            local += 1
    for chunk in chunks:
        for k in range(chunk.shape[0]):
            head[pl.ds(scalars[local], 1)] = chunk[k, : head.shape[1], :].astype(F32)[None]
            local += 1
    for a in range(rows):
        hole[:, a, :] = jnp.dot(
            hole_weights[...], head[:, a, :], precision=lax.Precision.HIGHEST,
            preferred_element_type=F32,
        )
    place, chosen = scalars[pairs + 1], scalars[pairs + 2]
    lanes = sums.shape[1]
    for i in range(local):
        term = hole[pl.ds(scalars[i], 1)][0, :rows, :]
        lane = lax.broadcasted_iota(jnp.int32, term.shape, 1)
        mask = (lane >= place) & (lane < place + width) & (chosen == 1)
        both = sums[i * rows : (i + 1) * rows] + jnp.where(mask, term, 0.0)
        both = both[:, : lanes // 2] + both[:, lanes // 2 :]
        both = both + pltpu.roll(both, 64, 1)
        both = both + pltpu.roll(both, 32, 1)
        other = pltpu.roll(both, 16, 1)
        row = lax.broadcasted_iota(jnp.int32, both.shape, 0)
        group = lax.broadcasted_iota(jnp.int32, both.shape, 1) // 16
        for h in range(2):
            tile = jnp.where(row % 2 == h, both, other)
            tile = jnp.sum(jnp.where(group == row, tile, 0.0), axis=0, keepdims=True)
            out[pl.ds(scalars[i] * 2 + h, 1)] = tile[None]


def per_device(amplitudes, factors, hole_weights, driver, eps_vir, pair_energy):
    pairs = hole_weights.shape[0]
    rows, columns = driver.shape[1], driver.shape[2]
    half = factors.shape[2] // 2
    width = factors.shape[1]
    x, ylo, yhi, z, core = (lax.axis_index(name) for name in AXES)
    aux_index = lax.axis_index(AUX)
    pair_index = lax.axis_index(PAIR)
    xs, lows = lax.axis_size("x"), lax.axis_size("ylo")

    own = amplitudes[0]
    split = jnp.stack([own[:, :half], own[:, half:]])
    sent = jnp.tile(split[None], (lax.axis_size("yhi") * lax.axis_size("z"), 1, 1, 1))
    amp = lax.all_to_all(sent.reshape(-1, *split.shape[1:]), AUX, 0, 0, tiled=True)
    amp = amp.reshape(-1, half)

    scattered = window_scattered(factors, rows)
    f_other = swapped(lax.dynamic_slice_in_dim(factors, (1 - core) * half, half, 2))
    amp, scattered = lax.optimization_barrier((amp, scattered))

    behind, ahead = shifted(amp, "y", 1), shifted(amp, "y", -1)
    window = window_collected(window_spread(scattered))
    opposite = shifted(behind, "y", 1)

    start = (aux_index * columns) % half
    here = lax.dynamic_slice_in_dim(amp[:rows], start, columns, 1)
    there = lax.dynamic_slice_in_dim(amp[:rows], start + columns * (1 - 2 * core), columns, 1)
    amp_cols = jnp.where(core == yhi, here, swapped(there)).astype(F32)

    chunk = jnp.stack([amp, behind, ahead, opposite])
    chunk, window, amp_cols = lax.optimization_barrier((chunk, window, amp_cols))
    window_other = swapped(window)
    x_behind, x_ahead = shifted(chunk, "x", 1), shifted(chunk, "x", -1)
    offsets = (0, 1, -1, 2)
    order = jnp.stack(
        [((x - i) % xs) * lows + (ylo - k) % lows for i in offsets for k in offsets]
    ).astype(jnp.int32)
    place = (pair_index * width) % half
    chosen = (yhi == 0) & (z == 0) & (core == (pair_index * width) // half)
    scalars = jnp.concatenate(
        [order, jnp.stack([core, place, chosen.astype(jnp.int32)]).astype(jnp.int32)]
    )

    head_rows = 8
    blocks = factors.shape[0] // BLOCK_Q
    span = rows * BLOCK_Q
    whole = pl.BlockSpec(memory_space=pltpu.VMEM)
    own_half = pl.BlockSpec((factors.shape[0], width, half), lambda i, s: (0, 0, s[pairs]))
    params = pltpu.CompilerParams(vmem_limit_bytes=40 * 1024 * 1024)

    def scratch(count):
        return pltpu.VMEM((count * span, 2 * blocks * half), BF16)

    def cost(count):
        return pl.CostEstimate(
            flops=605_000_000 * count, bytes_accessed=8_000_000, transcendentals=0
        )

    def early(*chunks):
        count = sum(c.shape[0] for c in chunks)
        return pl.pallas_call(
            early_kernel,
            grid_spec=pltpu.PrefetchScalarGridSpec(
                num_scalar_prefetch=1,
                grid=(1,),
                in_specs=[own_half] + [whole] * (3 + len(chunks)),
                out_specs=[whole, whole],
                scratch_shapes=[scratch(count)],
            ),
            out_shape=[
                jax.ShapeDtypeStruct((count * rows, BLOCK_Q * width), F32),
                jax.ShapeDtypeStruct((count, head_rows, half), F32),
            ],
            compiler_params=params,
            cost_estimate=cost(count),
        )(scalars, factors, f_other, window, window_other, *chunks)

    first = early(chunk)
    x_behind, x_ahead, first = lax.optimization_barrier((x_behind, x_ahead, first))
    cut = lows // 2
    last = (shifted(x_behind[:cut], "x", 1), shifted(x_ahead[cut:], "x", -1))
    done = [*first, *early(x_behind, x_ahead)]
    tiles = pl.pallas_call(
        lambda *refs: late_kernel(len(last), *refs),
        grid_spec=pltpu.PrefetchScalarGridSpec(
            num_scalar_prefetch=1,
            grid=(1,),
            in_specs=[own_half] + [whole] * (4 + len(last) + len(done)),
            out_specs=whole,
            scratch_shapes=[
                scratch(lows),
                pltpu.VMEM((pairs, head_rows, half), F32),
                pltpu.VMEM((pairs, head_rows, half), F32),
            ],
        ),
        out_shape=jax.ShapeDtypeStruct((pairs * 2, 1, 128), F32),
        compiler_params=params,
        cost_estimate=cost(lows),
    )(scalars, factors, f_other, window, window_other, hole_weights, *last, *done)

    summed = jnp.sum(lax.all_to_all(tiles, AUX, 0, 0, tiled=True), axis=0)
    count = lax.axis_size(AUX)
    parts = width // columns
    moves = []
    for g in range(pairs):
        for j in range(count):
            moves.append((g * count + j, (j // parts) * count + parts * g + j % parts))
    summed = lax.ppermute(summed, AXES, moves)
    summed = summed[:, : rows * columns].reshape(1, rows, columns)

    residual = driver + summed
    eps_cols = lax.dynamic_slice_in_dim(eps_vir, aux_index * columns, columns, 0)
    denominator = (
        eps_vir[:rows][None, :, None] + eps_cols[None, None, :] - pair_energy[:, None, None]
    )
    new_amps = amp_cols[None] - residual / denominator
    return (residual, new_amps)


def solution(mesh):
    finer = Mesh(mesh.devices.reshape(4, 4, 2, 8, 2), AXES)
    in_specs = (P(PAIR, AUX, None), P(AUX, PAIR, None), P(), P(PAIR, None, AUX), P(), P(PAIR))
    out_specs = (P(PAIR, None, AUX), P(PAIR, None, AUX))
    return jax.shard_map(
        per_device, mesh=finer, in_specs=in_specs, out_specs=out_specs, check_vma=False
    )
```

```python
import jax
import jax.numpy as jnp
from jax import lax
from jax.experimental import pallas as pl
from jax.experimental.pallas import tpu as pltpu
from jax.sharding import Mesh
from jax.sharding import PartitionSpec as P

AXES = ("x", "ylo", "yhi", "z", "core")
PAIR = ("x", "ylo")
AUX = ("yhi", "z", "core")
Y = ("ylo", "yhi")
BF16 = jnp.bfloat16
F32 = jnp.float32
BLOCK_Q = 8


def shifted(array, axis, by):
    if axis == "x":
        count = lax.axis_size("x")
        return lax.ppermute(array, "x", [(i, (i + by) % count) for i in range(count)])
    lows, highs = lax.axis_size("ylo"), lax.axis_size("yhi")

    def index(y):
        return (y % lows) * highs + y // lows

    full = lows * highs
    return lax.ppermute(array, Y, [(index(y), index((y + by) % full)) for y in range(full)])


def swapped(array):
    return lax.ppermute(array, "core", [(0, 1), (1, 0)])


def window_scattered(factors, rows):
    parts, lows = lax.axis_size("x"), lax.axis_size("ylo")
    wide = jnp.transpose(factors[:, :rows, :], (1, 0, 2))
    quarter = wide.shape[1] // parts
    pieces = [wide[:, i * quarter : (i + 1) * quarter, :] for i in range(parts)]
    first = (lax.axis_index("x") == 0) & (lax.axis_index("ylo") == 0)
    mine = jnp.where(first, pieces[0], jnp.zeros_like(pieces[0]))
    for i in range(1, parts):
        mine = mine + lax.ppermute(pieces[i], PAIR, [(0, i * lows)])
    return mine


def window_spread(mine):
    parts, lows = lax.axis_size("x"), lax.axis_size("ylo")
    return [
        lax.ppermute(mine, PAIR, [(i * lows, i * lows + k) for i in range(parts)])
        for k in range(1, lows)
    ]


def window_collected(mine, spread):
    quarter = jnp.where(lax.axis_index("ylo") == 0, mine, jnp.zeros_like(mine))
    for piece in spread:
        quarter = quarter + piece
    return collected(quarter)


def collected(array):
    parts = lax.axis_size("x")
    return lax.all_to_all(
        jnp.broadcast_to(array[None], (parts, *array.shape)), "x", 0, 0, tiled=True
    )


def own_half(scalars, factors, f_other, pairs):
    columns = f_other.shape[2]
    start = pl.multiple_of(scalars[pairs] * columns, columns)
    return factors.at[:, :, pl.ds(start, columns)]


def half_sums(f_own, f_other, w_own, w_other, chunks, halves):
    pieces, rows, per_piece, depth = w_own.shape
    per_piece = per_piece // BLOCK_Q
    blocks = pieces * per_piece
    columns = f_other.shape[2]
    span = rows * BLOCK_Q
    count = 0
    for chunk in chunks:
        for k in range(chunk.shape[0]):
            amp = chunk[k]
            for which, w in enumerate((w_own, w_other)):
                got = jnp.dot(
                    w[...].reshape(blocks * span, depth), amp, preferred_element_type=F32
                ).reshape(pieces, rows, per_piece, BLOCK_Q, columns)
                for piece in range(pieces):
                    for b in range(per_piece):
                        at = (which * blocks + piece * per_piece + b) * columns
                        halves[count * span : (count + 1) * span, at : at + columns] = (
                            got[piece, :, b].reshape(span, columns).astype(BF16)
                        )
            count += 1
    total = None
    group = 8
    for which, f in enumerate((f_own, f_other)):
        for start in range(0, blocks, group):
            right = jnp.concatenate(
                [
                    f[(start + b) * BLOCK_Q : (start + b + 1) * BLOCK_Q].reshape(-1, columns)
                    for b in range(group)
                ],
                axis=1,
            )
            at = (which * blocks + start) * columns
            term = lax.dot_general(
                halves[:, at : at + group * columns],
                right,
                (((1,), (1,)), ((), ())),
                preferred_element_type=F32,
            )
            total = term if total is None else total + term
    width = f_other.shape[1]
    total = total.reshape(count * rows, BLOCK_Q, BLOCK_Q * width)
    q = lax.broadcasted_iota(jnp.int32, total.shape, 1)
    lane = lax.broadcasted_iota(jnp.int32, total.shape, 2)
    return jnp.sum(jnp.where(lane // width == q, total, 0.0), axis=1)


def early_kernel(pairs, scalars, factors, f_other, w_own, w_other, *refs):
    chunks, (sums, heads, halves) = refs[:-3], refs[-3:]
    f_own = own_half(scalars, factors, f_other, pairs)
    sums[...] = half_sums(f_own, f_other, w_own, w_other, chunks, halves)
    count = 0
    for chunk in chunks:
        for k in range(chunk.shape[0]):
            heads[count] = chunk[k, : heads.shape[1], :].astype(F32)
            count += 1


def late_kernel(chunk_count, scalars, factors, f_other, w_own, w_other, hole_weights, *refs):
    chunks, refs = refs[:chunk_count], refs[chunk_count:]
    early, (out, halves, head, hole) = refs[:-4], refs[-4:]
    rows = w_own.shape[1]
    width = f_other.shape[1]
    pairs = hole_weights.shape[0]
    f_own = own_half(scalars, factors, f_other, pairs)
    sums = [s[...] for s in early[0::2]]
    sums.append(half_sums(f_own, f_other, w_own, w_other, chunks, halves))
    sums = jnp.concatenate(sums, axis=0)

    local = 0
    for heads in early[1::2]:
        for k in range(heads.shape[0]):
            head[pl.ds(scalars[local], 1)] = heads[k][None]
            local += 1
    for chunk in chunks:
        for k in range(chunk.shape[0]):
            head[pl.ds(scalars[local], 1)] = chunk[k, : head.shape[1], :].astype(F32)[None]
            local += 1
    for a in range(rows):
        hole[:, a, :] = jnp.dot(
            hole_weights[...], head[:, a, :], precision=lax.Precision.HIGHEST,
            preferred_element_type=F32,
        )
    place, chosen = scalars[pairs + 1], scalars[pairs + 2]
    lanes = sums.shape[1]
    for i in range(local):
        term = hole[pl.ds(scalars[i], 1)][0, :rows, :]
        lane = lax.broadcasted_iota(jnp.int32, term.shape, 1)
        mask = (lane >= place) & (lane < place + width) & (chosen == 1)
        both = sums[i * rows : (i + 1) * rows] + jnp.where(mask, term, 0.0)
        both = both[:, : lanes // 2] + both[:, lanes // 2 :]
        both = both + pltpu.roll(both, 64, 1)
        both = both + pltpu.roll(both, 32, 1)
        other = pltpu.roll(both, 16, 1)
        row = lax.broadcasted_iota(jnp.int32, both.shape, 0)
        group = lax.broadcasted_iota(jnp.int32, both.shape, 1) // 16
        for h in range(2):
            tile = jnp.where(row % 2 == h, both, other)
            tile = jnp.sum(jnp.where(group == row, tile, 0.0), axis=0, keepdims=True)
            out[pl.ds(scalars[i] * 2 + h, 1)] = tile[None]


def per_device(amplitudes, factors, hole_weights, driver, eps_vir, pair_energy):
    pairs = hole_weights.shape[0]
    rows, columns = driver.shape[1], driver.shape[2]
    half = factors.shape[2] // 2
    width = factors.shape[1]
    x, ylo, yhi, z, core = (lax.axis_index(name) for name in AXES)
    aux_index = lax.axis_index(AUX)
    pair_index = lax.axis_index(PAIR)
    xs, lows = lax.axis_size("x"), lax.axis_size("ylo")

    own = amplitudes[0]
    split = jnp.stack([own[:, :half], own[:, half:]])
    sent = jnp.tile(split[None], (lax.axis_size("yhi") * lax.axis_size("z"), 1, 1, 1))
    amp = lax.all_to_all(sent.reshape(-1, *split.shape[1:]), AUX, 0, 0, tiled=True)
    amp = amp.reshape(-1, half)

    scattered = window_scattered(factors, rows)
    amp, scattered = lax.optimization_barrier((amp, scattered))

    spread = window_spread(scattered)
    chunk = collected(amp)
    chunk, spread = lax.optimization_barrier((chunk, spread))
    behind, ahead = shifted(chunk, "y", 1), shifted(chunk, "y", -1)
    window = window_collected(scattered, spread)
    window_other = swapped(window)
    f_other = swapped(lax.dynamic_slice_in_dim(factors, (1 - core) * half, half, 2))

    start = (aux_index * columns) % half
    here = lax.dynamic_slice_in_dim(amp[:rows], start, columns, 1)
    there = lax.dynamic_slice_in_dim(amp[:rows], start + columns * (1 - 2 * core), columns, 1)
    amp_cols = jnp.where(core == yhi, here, swapped(there)).astype(F32)
    window_other, amp_cols, f_other = lax.optimization_barrier((window_other, amp_cols, f_other))

    order = jnp.stack(
        [i * lows + (ylo - k) % lows for k in (0, 1, -1, 2) for i in range(xs)]
    ).astype(jnp.int32)
    place = (pair_index * width) % half
    chosen = (yhi == 0) & (z == 0) & (core == (pair_index * width) // half)
    scalars = jnp.concatenate(
        [order, jnp.stack([core, place, chosen.astype(jnp.int32)]).astype(jnp.int32)]
    )

    head_rows = 8
    blocks = factors.shape[0] // BLOCK_Q
    span = rows * BLOCK_Q
    whole = pl.BlockSpec(memory_space=pltpu.VMEM)
    params = pltpu.CompilerParams(vmem_limit_bytes=44 * 1024 * 1024)

    def scratch(count):
        return pltpu.VMEM((count * span, 2 * blocks * half), BF16)

    def cost(count):
        return pl.CostEstimate(
            flops=605_000_000 * count, bytes_accessed=8_000_000, transcendentals=0
        )

    def early(*chunks):
        count = sum(c.shape[0] for c in chunks)
        return pl.pallas_call(
            lambda *refs: early_kernel(pairs, *refs),
            grid_spec=pltpu.PrefetchScalarGridSpec(
                num_scalar_prefetch=1,
                grid=(1,),
                in_specs=[whole] * (4 + len(chunks)),
                out_specs=[whole, whole],
                scratch_shapes=[scratch(count)],
            ),
            out_shape=[
                jax.ShapeDtypeStruct((count * rows, BLOCK_Q * width), F32),
                jax.ShapeDtypeStruct((count, head_rows, half), F32),
            ],
            compiler_params=params,
            cost_estimate=cost(count),
        )(scalars, factors, f_other, window, window_other, *chunks)

    first = early(chunk)
    behind, ahead, first = lax.optimization_barrier((behind, ahead, first))
    cut = xs // 2
    last = (shifted(behind[:cut], "y", 1), shifted(ahead[cut:], "y", -1))
    done = [*first, *early(behind, ahead)]
    tiles = pl.pallas_call(
        lambda *refs: late_kernel(len(last), *refs),
        grid_spec=pltpu.PrefetchScalarGridSpec(
            num_scalar_prefetch=1,
            grid=(1,),
            in_specs=[whole] * (5 + len(last) + len(done)),
            out_specs=whole,
            scratch_shapes=[
                scratch(lows),
                pltpu.VMEM((pairs, head_rows, half), F32),
                pltpu.VMEM((pairs, head_rows, half), F32),
            ],
        ),
        out_shape=jax.ShapeDtypeStruct((pairs * 2, 1, 128), F32),
        compiler_params=params,
        cost_estimate=cost(lows),
    )(scalars, factors, f_other, window, window_other, hole_weights, *last, *done)

    summed = jnp.sum(lax.all_to_all(tiles, AUX, 0, 0, tiled=True), axis=0)
    count = lax.axis_size(AUX)
    parts = width // columns
    moves = []
    for g in range(pairs):
        for j in range(count):
            moves.append((g * count + j, (j // parts) * count + parts * g + j % parts))
    summed = lax.ppermute(summed, AXES, moves)
    summed = summed[:, : rows * columns].reshape(1, rows, columns)

    residual = driver + summed
    eps_cols = lax.dynamic_slice_in_dim(eps_vir, aux_index * columns, columns, 0)
    denominator = (
        eps_vir[:rows][None, :, None] + eps_cols[None, None, :] - pair_energy[:, None, None]
    )
    new_amps = amp_cols[None] - residual / denominator
    return (residual, new_amps)


def solution(mesh):
    finer = Mesh(mesh.devices.reshape(4, 4, 2, 8, 2), AXES)
    in_specs = (P(PAIR, AUX, None), P(AUX, PAIR, None), P(), P(PAIR, None, AUX), P(), P(PAIR))
    out_specs = (P(PAIR, None, AUX), P(PAIR, None, AUX))
    return jax.shard_map(
        per_device, mesh=finer, in_specs=in_specs, out_specs=out_specs, check_vma=False
    )
```

```python
import jax
import jax.numpy as jnp
from jax import lax
from jax.experimental import pallas as pl
from jax.experimental.pallas import tpu as pltpu
from jax.sharding import Mesh
from jax.sharding import PartitionSpec as P

AXES = ("x", "ylo", "yhi", "z", "core")
PAIR = ("x", "ylo")
AUX = ("yhi", "z", "core")
Y = ("ylo", "yhi")
BF16 = jnp.bfloat16
F32 = jnp.float32
BLOCK_Q = 8


def shifted(array, axis, by):
    if axis == "x":
        count = lax.axis_size("x")
        return lax.ppermute(array, "x", [(i, (i + by) % count) for i in range(count)])
    lows, highs = lax.axis_size("ylo"), lax.axis_size("yhi")

    def index(y):
        return (y % lows) * highs + y // lows

    full = lows * highs
    return lax.ppermute(array, Y, [(index(y), index((y + by) % full)) for y in range(full)])


def swapped(array):
    return lax.ppermute(array, "core", [(0, 1), (1, 0)])


def window_scattered(factors, rows):
    parts, lows = lax.axis_size("x"), lax.axis_size("ylo")
    wide = jnp.transpose(factors[:, :rows, :], (1, 0, 2))
    quarter = wide.shape[1] // parts
    pieces = [wide[:, i * quarter : (i + 1) * quarter, :] for i in range(parts)]
    first = (lax.axis_index("x") == 0) & (lax.axis_index("ylo") == 0)
    mine = jnp.where(first, pieces[0], jnp.zeros_like(pieces[0]))
    for i in range(1, parts):
        mine = mine + lax.ppermute(pieces[i], PAIR, [(0, i * lows)])
    return mine


def window_spread(mine):
    parts, lows = lax.axis_size("x"), lax.axis_size("ylo")
    return [
        lax.ppermute(mine, PAIR, [(i * lows, i * lows + k) for i in range(parts)])
        for k in range(1, lows)
    ]


def window_quarter(mine, spread):
    quarter = jnp.where(lax.axis_index("ylo") == 0, mine, jnp.zeros_like(mine))
    for piece in spread:
        quarter = quarter + piece
    return quarter


def collected(array):
    parts = lax.axis_size("x")
    return lax.all_to_all(
        jnp.broadcast_to(array[None], (parts, *array.shape)), "x", 0, 0, tiled=True
    )


def fetched(scalars, pairs, factors, f_other, chunks, own, other, amps, arrived):
    columns = other.shape[2]
    start = pl.multiple_of(scalars[pairs] * columns, columns)
    taken, at = [], 0
    for i, chunk in enumerate(chunks):
        count = chunk.shape[0]
        taken.append(
            pltpu.make_async_copy(chunk, amps.at[at : at + count], arrived.at[2 + i])
        )
        at += count
    copies = (
        pltpu.make_async_copy(factors.at[:, :, pl.ds(start, columns)], own, arrived.at[0]),
        pltpu.make_async_copy(f_other, other, arrived.at[1]),
    )
    for copy in (*taken, *copies):
        copy.start()
    return taken, copies


def half_sums(taken, copies, f_own, f_other, w_own, w_other, chunks, amps, halves):
    pieces, rows, per_piece, depth = w_own.shape
    per_piece = per_piece // BLOCK_Q
    blocks = pieces * per_piece
    columns = f_other.shape[2]
    span = rows * BLOCK_Q
    count = 0
    for copy, chunk in zip(taken, chunks):
        copy.wait()
        for _ in range(chunk.shape[0]):
            amp = amps[count]
            for which, w in enumerate((w_own, w_other)):
                got = jnp.dot(
                    w[...].reshape(blocks * span, depth), amp, preferred_element_type=F32
                ).reshape(pieces, rows, per_piece, BLOCK_Q, columns)
                for piece in range(pieces):
                    for b in range(per_piece):
                        at = (which * blocks + piece * per_piece + b) * columns
                        halves[count * span : (count + 1) * span, at : at + columns] = (
                            got[piece, :, b].reshape(span, columns).astype(BF16)
                        )
            count += 1
    for copy in copies:
        copy.wait()
    total = None
    group = 8
    for which, f in enumerate((f_own, f_other)):
        for start in range(0, blocks, group):
            right = jnp.concatenate(
                [
                    f[(start + b) * BLOCK_Q : (start + b + 1) * BLOCK_Q].reshape(-1, columns)
                    for b in range(group)
                ],
                axis=1,
            )
            at = (which * blocks + start) * columns
            term = lax.dot_general(
                halves[:, at : at + group * columns],
                right,
                (((1,), (1,)), ((), ())),
                preferred_element_type=F32,
            )
            total = term if total is None else total + term
    width = f_other.shape[1]
    total = total.reshape(count * rows, BLOCK_Q, BLOCK_Q * width)
    q = lax.broadcasted_iota(jnp.int32, total.shape, 1)
    lane = lax.broadcasted_iota(jnp.int32, total.shape, 2)
    return jnp.sum(jnp.where(lane // width == q, total, 0.0), axis=1)


def early_kernel(pairs, scalars, factors, f_other, w_own, w_other, *refs):
    chunks, (sums, heads, halves, own, other, amps, arrived) = refs[:-7], refs[-7:]
    taken, copies = fetched(scalars, pairs, factors, f_other, chunks, own, other, amps, arrived)
    sums[...] = half_sums(taken, copies, own, other, w_own, w_other, chunks, amps, halves)
    heads[...] = amps[:, : heads.shape[1], :].astype(F32)


def late_kernel(chunk_count, scalars, factors, f_other, w_own, w_other, hole_weights, *refs):
    chunks, refs = refs[:chunk_count], refs[chunk_count:]
    early, (out, halves, own, other, amps, arrived, head, hole) = refs[:-8], refs[-8:]
    rows = w_own.shape[1]
    width = f_other.shape[1]
    pairs = hole_weights.shape[0]
    taken, copies = fetched(scalars, pairs, factors, f_other, chunks, own, other, amps, arrived)
    sums = [s[...] for s in early[0::2]]
    sums.append(half_sums(taken, copies, own, other, w_own, w_other, chunks, amps, halves))
    sums = jnp.concatenate(sums, axis=0)

    local = 0
    for heads in early[1::2]:
        for k in range(heads.shape[0]):
            head[pl.ds(scalars[local], 1)] = heads[k][None]
            local += 1
    for k in range(amps.shape[0]):
        head[pl.ds(scalars[local], 1)] = amps[k, : head.shape[1], :].astype(F32)[None]
        local += 1
    for a in range(rows):
        hole[:, a, :] = jnp.dot(
            hole_weights[...], head[:, a, :], precision=lax.Precision.HIGHEST,
            preferred_element_type=F32,
        )
    place, chosen = scalars[pairs + 1], scalars[pairs + 2]
    lanes = sums.shape[1]
    for i in range(local):
        term = hole[pl.ds(scalars[i], 1)][0, :rows, :]
        lane = lax.broadcasted_iota(jnp.int32, term.shape, 1)
        mask = (lane >= place) & (lane < place + width) & (chosen == 1)
        both = sums[i * rows : (i + 1) * rows] + jnp.where(mask, term, 0.0)
        both = both[:, : lanes // 2] + both[:, lanes // 2 :]
        both = both + pltpu.roll(both, 64, 1)
        both = both + pltpu.roll(both, 32, 1)
        other = pltpu.roll(both, 16, 1)
        row = lax.broadcasted_iota(jnp.int32, both.shape, 0)
        group = lax.broadcasted_iota(jnp.int32, both.shape, 1) // 16
        for h in range(2):
            tile = jnp.where(row % 2 == h, both, other)
            tile = jnp.sum(jnp.where(group == row, tile, 0.0), axis=0, keepdims=True)
            out[pl.ds(scalars[i] * 2 + h, 1)] = tile[None]


def per_device(amplitudes, factors, hole_weights, driver, eps_vir, pair_energy):
    pairs = hole_weights.shape[0]
    rows, columns = driver.shape[1], driver.shape[2]
    half = factors.shape[2] // 2
    width = factors.shape[1]
    x, ylo, yhi, z, core = (lax.axis_index(name) for name in AXES)
    aux_index = lax.axis_index(AUX)
    pair_index = lax.axis_index(PAIR)
    xs, lows = lax.axis_size("x"), lax.axis_size("ylo")

    own = amplitudes[0]
    split = jnp.stack([own[:, :half], own[:, half:]])
    sent = jnp.tile(split[None], (lax.axis_size("yhi") * lax.axis_size("z"), 1, 1, 1))
    amp = lax.all_to_all(sent.reshape(-1, *split.shape[1:]), AUX, 0, 0, tiled=True)
    amp = amp.reshape(-1, half)

    scattered = window_scattered(factors, rows)
    f_other = lax.dynamic_slice_in_dim(factors, (1 - core) * half, half, 2)
    amp, scattered, f_other = lax.optimization_barrier((amp, scattered, f_other))
    f_other = swapped(f_other)

    spread = window_spread(scattered)
    chunk = collected(amp)
    chunk, spread[0] = lax.optimization_barrier((chunk, spread[0]))
    behind, ahead = shifted(chunk, "y", 1), shifted(chunk, "y", -1)
    window = collected(window_quarter(scattered, spread))
    window_other = swapped(window)

    start = (aux_index * columns) % half
    here = lax.dynamic_slice_in_dim(amp[:rows], start, columns, 1)
    there = lax.dynamic_slice_in_dim(amp[:rows], start + columns * (1 - 2 * core), columns, 1)
    amp_cols = jnp.where(core == yhi, here, swapped(there)).astype(F32)
    window_other, amp_cols, f_other = lax.optimization_barrier((window_other, amp_cols, f_other))

    order = jnp.stack(
        [i * lows + (ylo - k) % lows for k in (0, 1, -1, 2) for i in range(xs)]
    ).astype(jnp.int32)
    place = (pair_index * width) % half
    chosen = (yhi == 0) & (z == 0) & (core == (pair_index * width) // half)
    scalars = jnp.concatenate(
        [order, jnp.stack([core, place, chosen.astype(jnp.int32)]).astype(jnp.int32)]
    )

    head_rows = 8
    blocks = factors.shape[0] // BLOCK_Q
    span = rows * BLOCK_Q
    whole = pl.BlockSpec(memory_space=pltpu.VMEM)
    afar = pl.BlockSpec(memory_space=pltpu.HBM)
    params = pltpu.CompilerParams(vmem_limit_bytes=56 * 1024 * 1024)

    def scratch(count, arrays):
        block = pltpu.VMEM((factors.shape[0], width, half), BF16)
        kept = pltpu.VMEM((count * span, 2 * blocks * half), BF16)
        amps = pltpu.VMEM((count, *amp.shape), BF16)
        return [kept, block, block, amps, pltpu.SemaphoreType.DMA((2 + arrays,))]

    def cost(count):
        return pl.CostEstimate(
            flops=1_000_000 * count, bytes_accessed=100_000, transcendentals=0
        )

    def early(*chunks):
        count = sum(c.shape[0] for c in chunks)
        return pl.pallas_call(
            lambda *refs: early_kernel(pairs, *refs),
            grid_spec=pltpu.PrefetchScalarGridSpec(
                num_scalar_prefetch=1,
                grid=(1,),
                in_specs=[afar, afar, whole, whole] + [afar] * len(chunks),
                out_specs=[whole, whole],
                scratch_shapes=scratch(count, len(chunks)),
            ),
            out_shape=[
                jax.ShapeDtypeStruct((count * rows, BLOCK_Q * width), F32),
                jax.ShapeDtypeStruct((count, head_rows, half), F32),
            ],
            compiler_params=params,
            cost_estimate=cost(count),
        )(scalars, factors, f_other, window, window_other, *chunks)

    cut = xs // 2
    last = (shifted(behind[:cut], "y", 1), shifted(ahead[cut:], "y", -1))
    done = early(chunk, behind, ahead)
    tiles = pl.pallas_call(
        lambda *refs: late_kernel(len(last), *refs),
        grid_spec=pltpu.PrefetchScalarGridSpec(
            num_scalar_prefetch=1,
            grid=(1,),
            in_specs=[afar, afar, whole, whole, whole]
            + [afar] * len(last)
            + [whole] * len(done),
            out_specs=whole,
            scratch_shapes=[
                *scratch(lows, len(last)),
                pltpu.VMEM((pairs, head_rows, half), F32),
                pltpu.VMEM((pairs, head_rows, half), F32),
            ],
        ),
        out_shape=jax.ShapeDtypeStruct((pairs * 2, 1, 128), F32),
        compiler_params=params,
        cost_estimate=cost(lows),
    )(scalars, factors, f_other, window, window_other, hole_weights, *last, *done)

    summed = jnp.sum(lax.all_to_all(tiles, AUX, 0, 0, tiled=True), axis=0)
    count = lax.axis_size(AUX)
    parts = width // columns
    moves = []
    for g in range(pairs):
        for j in range(count):
            moves.append((g * count + j, (j // parts) * count + parts * g + j % parts))
    summed = lax.ppermute(summed, AXES, moves)
    summed = summed[:, : rows * columns].reshape(1, rows, columns)

    residual = driver + summed
    eps_cols = lax.dynamic_slice_in_dim(eps_vir, aux_index * columns, columns, 0)
    denominator = (
        eps_vir[:rows][None, :, None] + eps_cols[None, None, :] - pair_energy[:, None, None]
    )
    new_amps = amp_cols[None] - residual / denominator
    return (residual, new_amps)


def solution(mesh):
    finer = Mesh(mesh.devices.reshape(4, 4, 2, 8, 2), AXES)
    in_specs = (P(PAIR, AUX, None), P(AUX, PAIR, None), P(), P(PAIR, None, AUX), P(), P(PAIR))
    out_specs = (P(PAIR, None, AUX), P(PAIR, None, AUX))
    return jax.shard_map(
        per_device, mesh=finer, in_specs=in_specs, out_specs=out_specs, check_vma=False
    )
```

```python
import jax
import jax.numpy as jnp
from jax import lax
from jax.experimental import pallas as pl
from jax.experimental.pallas import tpu as pltpu
from jax.sharding import Mesh
from jax.sharding import PartitionSpec as P

AXES = ("x", "ylo", "yhi", "z", "core")
PAIR = ("x", "ylo")
AUX = ("yhi", "z", "core")
Y = ("ylo", "yhi")
BF16 = jnp.bfloat16
F32 = jnp.float32
BLOCK_Q = 8


def shifted(array, axis, by):
    if axis == "x":
        count = lax.axis_size("x")
        return lax.ppermute(array, "x", [(i, (i + by) % count) for i in range(count)])
    lows, highs = lax.axis_size("ylo"), lax.axis_size("yhi")

    def index(y):
        return (y % lows) * highs + y // lows

    full = lows * highs
    return lax.ppermute(array, Y, [(index(y), index((y + by) % full)) for y in range(full)])


def swapped(array):
    return lax.ppermute(array, "core", [(0, 1), (1, 0)])


def window_scattered(factors, rows):
    parts, lows = lax.axis_size("x"), lax.axis_size("ylo")
    wide = jnp.transpose(factors[:, :rows, :], (1, 0, 2))
    quarter = wide.shape[1] // parts
    pieces = [wide[:, i * quarter : (i + 1) * quarter, :] for i in range(parts)]
    first = (lax.axis_index("x") == 0) & (lax.axis_index("ylo") == 0)
    mine = jnp.where(first, pieces[0], jnp.zeros_like(pieces[0]))
    for i in range(1, parts):
        mine = mine + lax.ppermute(pieces[i], PAIR, [(0, i * lows)])
    return mine


def window_spread(mine):
    parts, lows = lax.axis_size("x"), lax.axis_size("ylo")
    return [
        lax.ppermute(mine, PAIR, [(i * lows, i * lows + k) for i in range(parts)])
        for k in range(1, lows)
    ]


def window_quarter(mine, spread):
    quarter = jnp.where(lax.axis_index("ylo") == 0, mine, jnp.zeros_like(mine))
    for piece in spread:
        quarter = quarter + piece
    return quarter


def collected(array):
    parts = lax.axis_size("x")
    return lax.all_to_all(
        jnp.broadcast_to(array[None], (parts, *array.shape)), "x", 0, 0, tiled=True
    )


def half_sums(f_own, f_other, w_own, w_other, chunks, halves):
    pieces, rows, per_piece, depth = w_own.shape
    per_piece = per_piece // BLOCK_Q
    blocks = pieces * per_piece
    columns = f_other.shape[2]
    span = rows * BLOCK_Q
    count = 0
    for chunk in chunks:
        for k in range(chunk.shape[0]):
            amp = chunk[k]
            for which, w in enumerate((w_own, w_other)):
                got = jnp.dot(
                    w[...].reshape(blocks * span, depth), amp, preferred_element_type=F32
                ).reshape(pieces, rows, per_piece, BLOCK_Q, columns)
                for piece in range(pieces):
                    for b in range(per_piece):
                        at = (which * blocks + piece * per_piece + b) * columns
                        halves[count * span : (count + 1) * span, at : at + columns] = (
                            got[piece, :, b].reshape(span, columns).astype(BF16)
                        )
            count += 1
    total = None
    group = 8
    for which, f in enumerate((f_own, f_other)):
        for start in range(0, blocks, group):
            right = jnp.concatenate(
                [
                    f[(start + b) * BLOCK_Q : (start + b + 1) * BLOCK_Q].reshape(-1, columns)
                    for b in range(group)
                ],
                axis=1,
            )
            at = (which * blocks + start) * columns
            term = lax.dot_general(
                halves[:, at : at + group * columns],
                right,
                (((1,), (1,)), ((), ())),
                preferred_element_type=F32,
            )
            total = term if total is None else total + term
    width = f_other.shape[1]
    total = total.reshape(count * rows, BLOCK_Q, BLOCK_Q * width)
    q = lax.broadcasted_iota(jnp.int32, total.shape, 1)
    lane = lax.broadcasted_iota(jnp.int32, total.shape, 2)
    return jnp.sum(jnp.where(lane // width == q, total, 0.0), axis=1)


def early_kernel(scalars, f_own, f_other, w_own, w_other, *refs):
    chunks, (sums, heads, halves) = refs[:-3], refs[-3:]
    sums[...] = half_sums(f_own, f_other, w_own, w_other, chunks, halves)
    count = 0
    for chunk in chunks:
        for k in range(chunk.shape[0]):
            heads[count] = chunk[k, : heads.shape[1], :].astype(F32)
            count += 1


def late_kernel(chunk_count, scalars, f_own, f_other, w_own, w_other, hole_weights, *refs):
    chunks, refs = refs[:chunk_count], refs[chunk_count:]
    early, (out, halves, head, hole) = refs[:-4], refs[-4:]
    rows = w_own.shape[1]
    width = f_other.shape[1]
    pairs = hole_weights.shape[0]
    sums = [s[...] for s in early[0::2]]
    sums.append(half_sums(f_own, f_other, w_own, w_other, chunks, halves))
    sums = jnp.concatenate(sums, axis=0)

    local = 0
    for heads in early[1::2]:
        for k in range(heads.shape[0]):
            head[pl.ds(scalars[local], 1)] = heads[k][None]
            local += 1
    for chunk in chunks:
        for k in range(chunk.shape[0]):
            head[pl.ds(scalars[local], 1)] = chunk[k, : head.shape[1], :].astype(F32)[None]
            local += 1
    for a in range(rows):
        hole[:, a, :] = jnp.dot(
            hole_weights[...], head[:, a, :], precision=lax.Precision.HIGHEST,
            preferred_element_type=F32,
        )
    place, chosen = scalars[pairs + 1], scalars[pairs + 2]
    lanes = sums.shape[1]
    for i in range(local):
        term = hole[pl.ds(scalars[i], 1)][0, :rows, :]
        lane = lax.broadcasted_iota(jnp.int32, term.shape, 1)
        mask = (lane >= place) & (lane < place + width) & (chosen == 1)
        both = sums[i * rows : (i + 1) * rows] + jnp.where(mask, term, 0.0)
        both = both[:, : lanes // 2] + both[:, lanes // 2 :]
        both = both + pltpu.roll(both, 64, 1)
        both = both + pltpu.roll(both, 32, 1)
        other = pltpu.roll(both, 16, 1)
        row = lax.broadcasted_iota(jnp.int32, both.shape, 0)
        group = lax.broadcasted_iota(jnp.int32, both.shape, 1) // 16
        for h in range(2):
            tile = jnp.where(row % 2 == h, both, other)
            tile = jnp.sum(jnp.where(group == row, tile, 0.0), axis=0, keepdims=True)
            out[pl.ds(scalars[i] * 2 + h, 1)] = tile[None]


def per_device(amplitudes, factors, hole_weights, driver, eps_vir, pair_energy):
    pairs = hole_weights.shape[0]
    rows, columns = driver.shape[1], driver.shape[2]
    half = factors.shape[2] // 2
    width = factors.shape[1]
    x, ylo, yhi, z, core = (lax.axis_index(name) for name in AXES)
    aux_index = lax.axis_index(AUX)
    pair_index = lax.axis_index(PAIR)
    xs, lows = lax.axis_size("x"), lax.axis_size("ylo")

    own = amplitudes[0]
    split = jnp.stack([own[:, :half], own[:, half:]])
    sent = jnp.tile(split[None], (lax.axis_size("yhi") * lax.axis_size("z"), 1, 1, 1))
    amp = lax.all_to_all(sent.reshape(-1, *split.shape[1:]), AUX, 0, 0, tiled=True)
    amp = amp.reshape(-1, half)

    scattered = window_scattered(factors, rows)
    f_other = lax.dynamic_slice_in_dim(factors, (1 - core) * half, half, 2)
    amp, scattered, f_other = lax.optimization_barrier((amp, scattered, f_other))
    f_other = swapped(f_other)

    start = (aux_index * columns) % half
    here = lax.dynamic_slice_in_dim(amp[:rows], start, columns, 1)
    there = lax.dynamic_slice_in_dim(amp[:rows], start + columns * (1 - 2 * core), columns, 1)
    amp_cols = jnp.where(core == yhi, here, swapped(there)).astype(F32)

    order = jnp.stack(
        [i * lows + (ylo - k) % lows for k in (0, 1, -1, 2) for i in range(xs)]
    ).astype(jnp.int32)
    place = (pair_index * width) % half
    chosen = (yhi == 0) & (z == 0) & (core == (pair_index * width) // half)
    scalars = jnp.concatenate(
        [order, jnp.stack([core, place, chosen.astype(jnp.int32)]).astype(jnp.int32)]
    )

    spread = window_spread(scattered)
    chunk = collected(amp)
    chunk, spread[0], amp_cols, scalars = lax.optimization_barrier(
        (chunk, spread[0], amp_cols, scalars)
    )
    behind, ahead = shifted(chunk, "y", 1), shifted(chunk, "y", -1)
    window = collected(window_quarter(scattered, spread))
    window_other = swapped(window)

    head_rows = 8
    blocks = factors.shape[0] // BLOCK_Q
    span = rows * BLOCK_Q
    whole = pl.BlockSpec(memory_space=pltpu.VMEM)
    own_half = pl.BlockSpec((factors.shape[0], width, half), lambda i, s: (0, 0, s[pairs]))
    params = pltpu.CompilerParams(vmem_limit_bytes=44 * 1024 * 1024)

    def scratch(count):
        return pltpu.VMEM((count * span, 2 * blocks * half), BF16)

    def cost(count):
        return pl.CostEstimate(
            flops=1_000_000 * count, bytes_accessed=100_000, transcendentals=0
        )

    def early(*chunks):
        count = sum(c.shape[0] for c in chunks)
        return pl.pallas_call(
            early_kernel,
            grid_spec=pltpu.PrefetchScalarGridSpec(
                num_scalar_prefetch=1,
                grid=(1,),
                in_specs=[own_half] + [whole] * (3 + len(chunks)),
                out_specs=[whole, whole],
                scratch_shapes=[scratch(count)],
            ),
            out_shape=[
                jax.ShapeDtypeStruct((count * rows, BLOCK_Q * width), F32),
                jax.ShapeDtypeStruct((count, head_rows, half), F32),
            ],
            compiler_params=params,
            cost_estimate=cost(count),
        )(scalars, factors, f_other, window, window_other, *chunks)

    cut = xs // 2
    last = (shifted(behind[:cut], "y", 1), shifted(ahead[cut:], "y", -1))
    done = early(chunk, behind, ahead)
    tiles = pl.pallas_call(
        lambda *refs: late_kernel(len(last), *refs),
        grid_spec=pltpu.PrefetchScalarGridSpec(
            num_scalar_prefetch=1,
            grid=(1,),
            in_specs=[own_half] + [whole] * (4 + len(last) + len(done)),
            out_specs=whole,
            scratch_shapes=[
                scratch(lows),
                pltpu.VMEM((pairs, head_rows, half), F32),
                pltpu.VMEM((pairs, head_rows, half), F32),
            ],
        ),
        out_shape=jax.ShapeDtypeStruct((pairs * 2, 1, 128), F32),
        compiler_params=params,
        cost_estimate=cost(lows),
    )(scalars, factors, f_other, window, window_other, hole_weights, *last, *done)

    summed = jnp.sum(lax.all_to_all(tiles, AUX, 0, 0, tiled=True), axis=0)
    count = lax.axis_size(AUX)
    parts = width // columns
    moves = []
    for g in range(pairs):
        for j in range(count):
            moves.append((g * count + j, (j // parts) * count + parts * g + j % parts))
    summed = lax.ppermute(summed, AXES, moves)
    summed = summed[:, : rows * columns].reshape(1, rows, columns)

    residual = driver + summed
    eps_cols = lax.dynamic_slice_in_dim(eps_vir, aux_index * columns, columns, 0)
    denominator = (
        eps_vir[:rows][None, :, None] + eps_cols[None, None, :] - pair_energy[:, None, None]
    )
    new_amps = amp_cols[None] - residual / denominator
    return (residual, new_amps)


def solution(mesh):
    finer = Mesh(mesh.devices.reshape(4, 4, 2, 8, 2), AXES)
    in_specs = (P(PAIR, AUX, None), P(AUX, PAIR, None), P(), P(PAIR, None, AUX), P(), P(PAIR))
    out_specs = (P(PAIR, None, AUX), P(PAIR, None, AUX))
    return jax.shard_map(
        per_device, mesh=finer, in_specs=in_specs, out_specs=out_specs, check_vma=False
    )
```

```python
import jax
import jax.numpy as jnp
from jax import lax
from jax.experimental import pallas as pl
from jax.experimental.pallas import tpu as pltpu
from jax.sharding import Mesh
from jax.sharding import PartitionSpec as P

AXES = ("x", "ylo", "yhi", "z", "core")
PAIR = ("x", "ylo")
AUX = ("yhi", "z", "core")
Y = ("ylo", "yhi")
BF16 = jnp.bfloat16
F32 = jnp.float32
BLOCK_Q = 8


def shifted(array, axis, by):
    if axis == "x":
        count = lax.axis_size("x")
        return lax.ppermute(array, "x", [(i, (i + by) % count) for i in range(count)])
    lows, highs = lax.axis_size("ylo"), lax.axis_size("yhi")

    def index(y):
        return (y % lows) * highs + y // lows

    full = lows * highs
    return lax.ppermute(array, Y, [(index(y), index((y + by) % full)) for y in range(full)])


def swapped(array):
    return lax.ppermute(array, "core", [(0, 1), (1, 0)])


def window_scattered(factors, rows):
    parts, lows = lax.axis_size("x"), lax.axis_size("ylo")
    wide = jnp.transpose(factors[:, :rows, :], (1, 0, 2))
    quarter = wide.shape[1] // parts
    pieces = [wide[:, i * quarter : (i + 1) * quarter, :] for i in range(parts)]
    first = (lax.axis_index("x") == 0) & (lax.axis_index("ylo") == 0)
    mine = jnp.where(first, pieces[0], jnp.zeros_like(pieces[0]))
    for i in range(1, parts):
        mine = mine + lax.ppermute(pieces[i], PAIR, [(0, i * lows)])
    return mine


def window_spread(mine):
    parts, lows = lax.axis_size("x"), lax.axis_size("ylo")
    return [
        lax.ppermute(mine, PAIR, [(i * lows, i * lows + k) for i in range(parts)])
        for k in range(1, lows)
    ]


def window_quarter(mine, spread):
    quarter = jnp.where(lax.axis_index("ylo") == 0, mine, jnp.zeros_like(mine))
    for piece in spread:
        quarter = quarter + piece
    return quarter


def collected(array):
    parts = lax.axis_size("x")
    return lax.all_to_all(
        jnp.broadcast_to(array[None], (parts, *array.shape)), "x", 0, 0, tiled=True
    )


def half_sums(f_own, f_other, w_own, w_other, chunks, halves):
    pieces, rows, per_piece, depth = w_own.shape
    per_piece = per_piece // BLOCK_Q
    blocks = pieces * per_piece
    columns = f_other.shape[2]
    span = rows * BLOCK_Q
    count = 0
    for chunk in chunks:
        for k in range(chunk.shape[0]):
            amp = chunk[k]
            for which, w in enumerate((w_own, w_other)):
                got = jnp.dot(
                    w[...].reshape(blocks * span, depth), amp, preferred_element_type=F32
                ).reshape(pieces, rows, per_piece, BLOCK_Q, columns)
                for piece in range(pieces):
                    for b in range(per_piece):
                        at = (which * blocks + piece * per_piece + b) * columns
                        halves[count * span : (count + 1) * span, at : at + columns] = (
                            got[piece, :, b].reshape(span, columns).astype(BF16)
                        )
            count += 1
    total = None
    group = 8
    for which, f in enumerate((f_own, f_other)):
        for start in range(0, blocks, group):
            right = jnp.concatenate(
                [
                    f[(start + b) * BLOCK_Q : (start + b + 1) * BLOCK_Q].reshape(-1, columns)
                    for b in range(group)
                ],
                axis=1,
            )
            at = (which * blocks + start) * columns
            term = lax.dot_general(
                halves[:, at : at + group * columns],
                right,
                (((1,), (1,)), ((), ())),
                preferred_element_type=F32,
            )
            total = term if total is None else total + term
    width = f_other.shape[1]
    total = total.reshape(count * rows, BLOCK_Q, BLOCK_Q * width)
    q = lax.broadcasted_iota(jnp.int32, total.shape, 1)
    lane = lax.broadcasted_iota(jnp.int32, total.shape, 2)
    return jnp.sum(jnp.where(lane // width == q, total, 0.0), axis=1)


def early_kernel(scalars, f_own, f_other, w_own, w_other, *refs):
    chunks, (sums, heads, halves) = refs[:-3], refs[-3:]
    sums[...] = half_sums(f_own, f_other, w_own, w_other, chunks, halves)
    count = 0
    for chunk in chunks:
        for k in range(chunk.shape[0]):
            heads[count] = chunk[k, : heads.shape[1], :].astype(F32)
            count += 1


def late_kernel(chunk_count, scalars, f_own, f_other, w_own, w_other, hole_weights, *refs):
    chunks, refs = refs[:chunk_count], refs[chunk_count:]
    early, (out, halves, head, hole) = refs[:-4], refs[-4:]
    rows = w_own.shape[1]
    width = f_other.shape[1]
    pairs = hole_weights.shape[0]
    sums = [s[...] for s in early[0::2]]
    sums.append(half_sums(f_own, f_other, w_own, w_other, chunks, halves))
    sums = jnp.concatenate(sums, axis=0)

    local = 0
    for heads in early[1::2]:
        for k in range(heads.shape[0]):
            head[pl.ds(scalars[local], 1)] = heads[k][None]
            local += 1
    for chunk in chunks:
        for k in range(chunk.shape[0]):
            head[pl.ds(scalars[local], 1)] = chunk[k, : head.shape[1], :].astype(F32)[None]
            local += 1
    for a in range(rows):
        hole[:, a, :] = jnp.dot(
            hole_weights[...], head[:, a, :], precision=lax.Precision.HIGHEST,
            preferred_element_type=F32,
        )
    place, chosen = scalars[pairs + 1], scalars[pairs + 2]
    lanes = sums.shape[1]
    for i in range(local):
        term = hole[pl.ds(scalars[i], 1)][0, :rows, :]
        lane = lax.broadcasted_iota(jnp.int32, term.shape, 1)
        mask = (lane >= place) & (lane < place + width) & (chosen == 1)
        both = sums[i * rows : (i + 1) * rows] + jnp.where(mask, term, 0.0)
        both = both[:, : lanes // 2] + both[:, lanes // 2 :]
        both = both + pltpu.roll(both, 64, 1)
        both = both + pltpu.roll(both, 32, 1)
        other = pltpu.roll(both, 16, 1)
        row = lax.broadcasted_iota(jnp.int32, both.shape, 0)
        group = lax.broadcasted_iota(jnp.int32, both.shape, 1) // 16
        for h in range(2):
            tile = jnp.where(row % 2 == h, both, other)
            tile = jnp.sum(jnp.where(group == row, tile, 0.0), axis=0, keepdims=True)
            out[pl.ds(scalars[i] * 2 + h, 1)] = tile[None]


def per_device(amplitudes, factors, hole_weights, driver, eps_vir, pair_energy):
    pairs = hole_weights.shape[0]
    rows, columns = driver.shape[1], driver.shape[2]
    half = factors.shape[2] // 2
    width = factors.shape[1]
    x, ylo, yhi, z, core = (lax.axis_index(name) for name in AXES)
    aux_index = lax.axis_index(AUX)
    pair_index = lax.axis_index(PAIR)
    xs, lows = lax.axis_size("x"), lax.axis_size("ylo")

    own = amplitudes[0]
    split = jnp.stack([own[:, :half], own[:, half:]])
    sent = jnp.tile(split[None], (lax.axis_size("yhi") * lax.axis_size("z"), 1, 1, 1))
    amp = lax.all_to_all(sent.reshape(-1, *split.shape[1:]), AUX, 0, 0, tiled=True)
    amp = amp.reshape(-1, half)

    scattered = window_scattered(factors, rows)
    f_other = lax.dynamic_slice_in_dim(factors, (1 - core) * half, half, 2)
    amp, f_other = lax.optimization_barrier((amp, f_other))
    f_other = swapped(f_other)

    start = (aux_index * columns) % half
    here = lax.dynamic_slice_in_dim(amp[:rows], start, columns, 1)
    there = lax.dynamic_slice_in_dim(amp[:rows], start + columns * (1 - 2 * core), columns, 1)
    amp_cols = jnp.where(core == yhi, here, swapped(there)).astype(F32)

    order = jnp.stack(
        [i * lows + (ylo - k) % lows for k in (0, 1, -1, 2) for i in range(xs)]
    ).astype(jnp.int32)
    place = (pair_index * width) % half
    chosen = (yhi == 0) & (z == 0) & (core == (pair_index * width) // half)
    scalars = jnp.concatenate(
        [order, jnp.stack([core, place, chosen.astype(jnp.int32)]).astype(jnp.int32)]
    )

    spread = window_spread(scattered)
    chunk = collected(amp)
    chunk, spread[0], amp_cols, scalars = lax.optimization_barrier(
        (chunk, spread[0], amp_cols, scalars)
    )
    behind, ahead = shifted(chunk, "y", 1), shifted(chunk, "y", -1)
    window = collected(window_quarter(scattered, spread))
    window_other = swapped(window)

    head_rows = 8
    blocks = factors.shape[0] // BLOCK_Q
    span = rows * BLOCK_Q
    whole = pl.BlockSpec(memory_space=pltpu.VMEM)
    own_half = pl.BlockSpec((factors.shape[0], width, half), lambda i, s: (0, 0, s[pairs]))
    params = pltpu.CompilerParams(vmem_limit_bytes=44 * 1024 * 1024)

    def scratch(count):
        return pltpu.VMEM((count * span, 2 * blocks * half), BF16)

    def cost(count):
        return pl.CostEstimate(
            flops=1_000_000 * count, bytes_accessed=100_000, transcendentals=0
        )

    def early(*chunks):
        count = sum(c.shape[0] for c in chunks)
        return pl.pallas_call(
            early_kernel,
            grid_spec=pltpu.PrefetchScalarGridSpec(
                num_scalar_prefetch=1,
                grid=(1,),
                in_specs=[own_half] + [whole] * (3 + len(chunks)),
                out_specs=[whole, whole],
                scratch_shapes=[scratch(count)],
            ),
            out_shape=[
                jax.ShapeDtypeStruct((count * rows, BLOCK_Q * width), F32),
                jax.ShapeDtypeStruct((count, head_rows, half), F32),
            ],
            compiler_params=params,
            cost_estimate=cost(count),
        )(scalars, factors, f_other, window, window_other, *chunks)

    cut = xs // 2
    last = (shifted(behind[:cut], "y", 1), shifted(ahead[cut:], "y", -1))
    done = early(chunk, behind, ahead)
    tiles = pl.pallas_call(
        lambda *refs: late_kernel(len(last), *refs),
        grid_spec=pltpu.PrefetchScalarGridSpec(
            num_scalar_prefetch=1,
            grid=(1,),
            in_specs=[own_half] + [whole] * (4 + len(last) + len(done)),
            out_specs=whole,
            scratch_shapes=[
                scratch(lows),
                pltpu.VMEM((pairs, head_rows, half), F32),
                pltpu.VMEM((pairs, head_rows, half), F32),
            ],
        ),
        out_shape=jax.ShapeDtypeStruct((pairs * 2, 1, 128), F32),
        compiler_params=params,
        cost_estimate=cost(lows),
    )(scalars, factors, f_other, window, window_other, hole_weights, *last, *done)

    summed = jnp.sum(lax.all_to_all(tiles, AUX, 0, 0, tiled=True), axis=0)
    count = lax.axis_size(AUX)
    parts = width // columns
    moves = []
    for g in range(pairs):
        for j in range(count):
            moves.append((g * count + j, (j // parts) * count + parts * g + j % parts))
    summed = lax.ppermute(summed, AXES, moves)
    summed = summed[:, : rows * columns].reshape(1, rows, columns)

    residual = driver + summed
    eps_cols = lax.dynamic_slice_in_dim(eps_vir, aux_index * columns, columns, 0)
    denominator = (
        eps_vir[:rows][None, :, None] + eps_cols[None, None, :] - pair_energy[:, None, None]
    )
    new_amps = amp_cols[None] - residual / denominator
    return (residual, new_amps)


def solution(mesh):
    finer = Mesh(mesh.devices.reshape(4, 4, 2, 8, 2), AXES)
    in_specs = (P(PAIR, AUX, None), P(AUX, PAIR, None), P(), P(PAIR, None, AUX), P(), P(PAIR))
    out_specs = (P(PAIR, None, AUX), P(PAIR, None, AUX))
    return jax.shard_map(
        per_device, mesh=finer, in_specs=in_specs, out_specs=out_specs, check_vma=False
    )
```

```python
import jax
import jax.numpy as jnp
from jax import lax
from jax.experimental import pallas as pl
from jax.experimental.pallas import tpu as pltpu
from jax.sharding import Mesh
from jax.sharding import PartitionSpec as P

AXES = ("x", "ylo", "yhi", "z", "core")
PAIR = ("x", "ylo")
AUX = ("yhi", "z", "core")
Y = ("ylo", "yhi")
BF16 = jnp.bfloat16
F32 = jnp.float32
BLOCK_Q = 8


def shifted(array, axis, by):
    if axis == "x":
        count = lax.axis_size("x")
        return lax.ppermute(array, "x", [(i, (i + by) % count) for i in range(count)])
    lows, highs = lax.axis_size("ylo"), lax.axis_size("yhi")

    def index(y):
        return (y % lows) * highs + y // lows

    full = lows * highs
    return lax.ppermute(array, Y, [(index(y), index((y + by) % full)) for y in range(full)])


def swapped(array):
    return lax.ppermute(array, "core", [(0, 1), (1, 0)])


def window_scattered(factors, rows):
    parts, lows = lax.axis_size("x"), lax.axis_size("ylo")
    wide = jnp.transpose(factors[:, :rows, :], (1, 0, 2))
    quarter = wide.shape[1] // parts
    pieces = [wide[:, i * quarter : (i + 1) * quarter, :] for i in range(parts)]
    first = (lax.axis_index("x") == 0) & (lax.axis_index("ylo") == 0)
    mine = jnp.where(first, pieces[0], jnp.zeros_like(pieces[0]))
    for i in range(1, parts):
        mine = mine + lax.ppermute(pieces[i], PAIR, [(0, i * lows)])
    return mine


def window_spread(mine):
    parts, lows = lax.axis_size("x"), lax.axis_size("ylo")
    return [
        lax.ppermute(mine, PAIR, [(i * lows, i * lows + k) for i in range(parts)])
        for k in range(1, lows)
    ]


def window_quarter(mine, spread):
    quarter = jnp.where(lax.axis_index("ylo") == 0, mine, jnp.zeros_like(mine))
    for piece in spread:
        quarter = quarter + piece
    return quarter


def collected(array):
    parts = lax.axis_size("x")
    return lax.all_to_all(
        jnp.broadcast_to(array[None], (parts, *array.shape)), "x", 0, 0, tiled=True
    )


def half_sums(f_own, f_other, w_own, w_other, chunks, halves):
    pieces, rows, per_piece, depth = w_own.shape
    per_piece = per_piece // BLOCK_Q
    blocks = pieces * per_piece
    columns = f_other.shape[2]
    span = rows * BLOCK_Q
    count = 0
    for chunk in chunks:
        for k in range(chunk.shape[0]):
            amp = chunk[k]
            for which, w in enumerate((w_own, w_other)):
                got = jnp.dot(
                    w[...].reshape(blocks * span, depth), amp, preferred_element_type=F32
                ).reshape(pieces, rows, per_piece, BLOCK_Q, columns)
                for piece in range(pieces):
                    for b in range(per_piece):
                        at = (which * blocks + piece * per_piece + b) * columns
                        halves[count * span : (count + 1) * span, at : at + columns] = (
                            got[piece, :, b].reshape(span, columns).astype(BF16)
                        )
            count += 1
    total = None
    group = 8
    for which, f in enumerate((f_own, f_other)):
        for start in range(0, blocks, group):
            right = jnp.concatenate(
                [
                    f[(start + b) * BLOCK_Q : (start + b + 1) * BLOCK_Q].reshape(-1, columns)
                    for b in range(group)
                ],
                axis=1,
            )
            at = (which * blocks + start) * columns
            term = lax.dot_general(
                halves[:, at : at + group * columns],
                right,
                (((1,), (1,)), ((), ())),
                preferred_element_type=F32,
            )
            total = term if total is None else total + term
    width = f_other.shape[1]
    total = total.reshape(count * rows, BLOCK_Q, BLOCK_Q * width)
    q = lax.broadcasted_iota(jnp.int32, total.shape, 1)
    lane = lax.broadcasted_iota(jnp.int32, total.shape, 2)
    return jnp.sum(jnp.where(lane // width == q, total, 0.0), axis=1)


def early_kernel(scalars, f_own, f_other, w_own, w_other, *refs):
    chunks, (sums, heads, halves) = refs[:-3], refs[-3:]
    sums[...] = half_sums(f_own, f_other, w_own, w_other, chunks, halves)
    count = 0
    for chunk in chunks:
        for k in range(chunk.shape[0]):
            heads[count] = chunk[k, : heads.shape[1], :].astype(F32)
            count += 1


def late_kernel(chunk_count, scalars, f_own, f_other, w_own, w_other, hole_weights, *refs):
    chunks, refs = refs[:chunk_count], refs[chunk_count:]
    early, (out, halves, head, hole) = refs[:-4], refs[-4:]
    rows = w_own.shape[1]
    width = f_other.shape[1]
    pairs = hole_weights.shape[0]
    sums = [s[...] for s in early[0::2]]
    sums.append(half_sums(f_own, f_other, w_own, w_other, chunks, halves))
    sums = jnp.concatenate(sums, axis=0)

    local = 0
    for heads in early[1::2]:
        for k in range(heads.shape[0]):
            head[pl.ds(scalars[local], 1)] = heads[k][None]
            local += 1
    for chunk in chunks:
        for k in range(chunk.shape[0]):
            head[pl.ds(scalars[local], 1)] = chunk[k, : head.shape[1], :].astype(F32)[None]
            local += 1
    for a in range(rows):
        hole[:, a, :] = jnp.dot(
            hole_weights[...], head[:, a, :], precision=lax.Precision.HIGHEST,
            preferred_element_type=F32,
        )
    place, chosen = scalars[pairs + 1], scalars[pairs + 2]
    lanes = sums.shape[1]
    for i in range(local):
        term = hole[pl.ds(scalars[i], 1)][0, :rows, :]
        lane = lax.broadcasted_iota(jnp.int32, term.shape, 1)
        mask = (lane >= place) & (lane < place + width) & (chosen == 1)
        both = sums[i * rows : (i + 1) * rows] + jnp.where(mask, term, 0.0)
        both = both[:, : lanes // 2] + both[:, lanes // 2 :]
        both = both + pltpu.roll(both, 64, 1)
        both = both + pltpu.roll(both, 32, 1)
        other = pltpu.roll(both, 16, 1)
        row = lax.broadcasted_iota(jnp.int32, both.shape, 0)
        group = lax.broadcasted_iota(jnp.int32, both.shape, 1) // 16
        for h in range(2):
            tile = jnp.where(row % 2 == h, both, other)
            tile = jnp.sum(jnp.where(group == row, tile, 0.0), axis=0, keepdims=True)
            out[pl.ds(scalars[i] * 2 + h, 1)] = tile[None]


def per_device(amplitudes, factors, hole_weights, driver, eps_vir, pair_energy):
    pairs = hole_weights.shape[0]
    rows, columns = driver.shape[1], driver.shape[2]
    half = factors.shape[2] // 2
    width = factors.shape[1]
    x, ylo, yhi, z, core = (lax.axis_index(name) for name in AXES)
    aux_index = lax.axis_index(AUX)
    pair_index = lax.axis_index(PAIR)
    xs, lows = lax.axis_size("x"), lax.axis_size("ylo")

    own = amplitudes[0]
    split = jnp.stack([own[:, :half], own[:, half:]])
    sent = jnp.tile(split[None], (lax.axis_size("yhi") * lax.axis_size("z"), 1, 1, 1))
    amp = lax.all_to_all(sent.reshape(-1, *split.shape[1:]), AUX, 0, 0, tiled=True)
    amp = amp.reshape(-1, half)

    scattered = window_scattered(factors, rows)
    f_other = lax.dynamic_slice_in_dim(factors, (1 - core) * half, half, 2)
    amp, f_other = lax.optimization_barrier((amp, f_other))
    f_other = swapped(f_other)

    start = (aux_index * columns) % half
    here = lax.dynamic_slice_in_dim(amp[:rows], start, columns, 1)
    there = lax.dynamic_slice_in_dim(amp[:rows], start + columns * (1 - 2 * core), columns, 1)
    amp_cols = jnp.where(core == yhi, here, swapped(there)).astype(F32)

    order = jnp.stack(
        [i * lows + (ylo - k) % lows for k in (0, 1, -1, 2) for i in range(xs)]
    ).astype(jnp.int32)
    place = (pair_index * width) % half
    chosen = (yhi == 0) & (z == 0) & (core == (pair_index * width) // half)
    scalars = jnp.concatenate(
        [order, jnp.stack([core, place, chosen.astype(jnp.int32)]).astype(jnp.int32)]
    )

    spread = window_spread(scattered)
    chunk = collected(amp)
    chunk, amp_cols, scalars = lax.optimization_barrier((chunk, amp_cols, scalars))
    behind, ahead = shifted(chunk, "y", 1), shifted(chunk, "y", -1)
    window = collected(window_quarter(scattered, spread))
    window_other = swapped(window)

    head_rows = 8
    blocks = factors.shape[0] // BLOCK_Q
    span = rows * BLOCK_Q
    whole = pl.BlockSpec(memory_space=pltpu.VMEM)
    own_half = pl.BlockSpec((factors.shape[0], width, half), lambda i, s: (0, 0, s[pairs]))
    params = pltpu.CompilerParams(vmem_limit_bytes=44 * 1024 * 1024)

    def scratch(count):
        return pltpu.VMEM((count * span, 2 * blocks * half), BF16)

    def cost(count):
        return pl.CostEstimate(
            flops=1_000_000 * count, bytes_accessed=100_000, transcendentals=0
        )

    def early(*chunks):
        count = sum(c.shape[0] for c in chunks)
        return pl.pallas_call(
            early_kernel,
            grid_spec=pltpu.PrefetchScalarGridSpec(
                num_scalar_prefetch=1,
                grid=(1,),
                in_specs=[own_half] + [whole] * (3 + len(chunks)),
                out_specs=[whole, whole],
                scratch_shapes=[scratch(count)],
            ),
            out_shape=[
                jax.ShapeDtypeStruct((count * rows, BLOCK_Q * width), F32),
                jax.ShapeDtypeStruct((count, head_rows, half), F32),
            ],
            compiler_params=params,
            cost_estimate=cost(count),
        )(scalars, factors, f_other, window, window_other, *chunks)

    cut = xs // 2
    last = (shifted(behind[:cut], "y", 1), shifted(ahead[cut:], "y", -1))
    done = early(chunk, behind, ahead)
    tiles = pl.pallas_call(
        lambda *refs: late_kernel(len(last), *refs),
        grid_spec=pltpu.PrefetchScalarGridSpec(
            num_scalar_prefetch=1,
            grid=(1,),
            in_specs=[own_half] + [whole] * (4 + len(last) + len(done)),
            out_specs=whole,
            scratch_shapes=[
                scratch(lows),
                pltpu.VMEM((pairs, head_rows, half), F32),
                pltpu.VMEM((pairs, head_rows, half), F32),
            ],
        ),
        out_shape=jax.ShapeDtypeStruct((pairs * 2, 1, 128), F32),
        compiler_params=params,
        cost_estimate=cost(lows),
    )(scalars, factors, f_other, window, window_other, hole_weights, *last, *done)

    summed = jnp.sum(lax.all_to_all(tiles, AUX, 0, 0, tiled=True), axis=0)
    count = lax.axis_size(AUX)
    parts = width // columns
    moves = []
    for g in range(pairs):
        for j in range(count):
            moves.append((g * count + j, (j // parts) * count + parts * g + j % parts))
    summed = lax.ppermute(summed, AXES, moves)
    summed = summed[:, : rows * columns].reshape(1, rows, columns)

    residual = driver + summed
    eps_cols = lax.dynamic_slice_in_dim(eps_vir, aux_index * columns, columns, 0)
    denominator = (
        eps_vir[:rows][None, :, None] + eps_cols[None, None, :] - pair_energy[:, None, None]
    )
    new_amps = amp_cols[None] - residual / denominator
    return (residual, new_amps)


def solution(mesh):
    finer = Mesh(mesh.devices.reshape(4, 4, 2, 8, 2), AXES)
    in_specs = (P(PAIR, AUX, None), P(AUX, PAIR, None), P(), P(PAIR, None, AUX), P(), P(PAIR))
    out_specs = (P(PAIR, None, AUX), P(PAIR, None, AUX))
    return jax.shard_map(
        per_device, mesh=finer, in_specs=in_specs, out_specs=out_specs, check_vma=False
    )
```

```python
import jax
import jax.numpy as jnp
from jax import lax
from jax.experimental import pallas as pl
from jax.experimental.pallas import tpu as pltpu
from jax.sharding import Mesh
from jax.sharding import PartitionSpec as P

AXES = ("x", "ylo", "yhi", "z", "core")
PAIR = ("x", "ylo")
AUX = ("yhi", "z", "core")
Y = ("ylo", "yhi")
BF16 = jnp.bfloat16
F32 = jnp.float32
BLOCK_Q = 8


def shifted(array, axis, by):
    if axis == "x":
        count = lax.axis_size("x")
        return lax.ppermute(array, "x", [(i, (i + by) % count) for i in range(count)])
    lows, highs = lax.axis_size("ylo"), lax.axis_size("yhi")

    def index(y):
        return (y % lows) * highs + y // lows

    full = lows * highs
    return lax.ppermute(array, Y, [(index(y), index((y + by) % full)) for y in range(full)])


def swapped(array):
    return lax.ppermute(array, "core", [(0, 1), (1, 0)])


def window_scattered(factors, rows):
    parts, lows = lax.axis_size("x"), lax.axis_size("ylo")
    wide = jnp.transpose(factors[:, :rows, :], (1, 0, 2))
    quarter = wide.shape[1] // parts
    pieces = [wide[:, i * quarter : (i + 1) * quarter, :] for i in range(parts)]
    first = (lax.axis_index("x") == 0) & (lax.axis_index("ylo") == 0)
    mine = jnp.where(first, pieces[0], jnp.zeros_like(pieces[0]))
    for i in range(1, parts):
        mine = mine + lax.ppermute(pieces[i], PAIR, [(0, i * lows)])
    return mine


def window_spread(mine):
    parts, lows = lax.axis_size("x"), lax.axis_size("ylo")
    quarter = jnp.where(lax.axis_index("ylo") == 0, mine, jnp.zeros_like(mine))
    stride = lows // 2
    while stride:
        moves = [
            (i * lows + k, i * lows + k + stride)
            for i in range(parts)
            for k in range(0, lows, 2 * stride)
        ]
        quarter = quarter + lax.ppermute(quarter, PAIR, moves)
        stride //= 2
    return quarter


def collected(array):
    parts = lax.axis_size("x")
    return lax.all_to_all(
        jnp.broadcast_to(array[None], (parts, *array.shape)), "x", 0, 0, tiled=True
    )


def half_sums(f_own, f_other, w_own, w_other, chunks, halves):
    pieces, rows, per_piece, depth = w_own.shape
    per_piece = per_piece // BLOCK_Q
    blocks = pieces * per_piece
    columns = f_other.shape[2]
    span = rows * BLOCK_Q
    count = 0
    for chunk in chunks:
        for k in range(chunk.shape[0]):
            amp = chunk[k]
            for which, w in enumerate((w_own, w_other)):
                got = jnp.dot(
                    w[...].reshape(blocks * span, depth), amp, preferred_element_type=F32
                ).reshape(pieces, rows, per_piece, BLOCK_Q, columns)
                for piece in range(pieces):
                    for b in range(per_piece):
                        at = (which * blocks + piece * per_piece + b) * columns
                        halves[count * span : (count + 1) * span, at : at + columns] = (
                            got[piece, :, b].reshape(span, columns).astype(BF16)
                        )
            count += 1
    total = None
    group = 8
    for which, f in enumerate((f_own, f_other)):
        for start in range(0, blocks, group):
            right = jnp.concatenate(
                [
                    f[(start + b) * BLOCK_Q : (start + b + 1) * BLOCK_Q].reshape(-1, columns)
                    for b in range(group)
                ],
                axis=1,
            )
            at = (which * blocks + start) * columns
            term = lax.dot_general(
                halves[:, at : at + group * columns],
                right,
                (((1,), (1,)), ((), ())),
                preferred_element_type=F32,
            )
            total = term if total is None else total + term
    width = f_other.shape[1]
    total = total.reshape(count * rows, BLOCK_Q, BLOCK_Q * width)
    q = lax.broadcasted_iota(jnp.int32, total.shape, 1)
    lane = lax.broadcasted_iota(jnp.int32, total.shape, 2)
    return jnp.sum(jnp.where(lane // width == q, total, 0.0), axis=1)


def early_kernel(scalars, f_own, f_other, w_own, w_other, *refs):
    chunks, (sums, heads, halves) = refs[:-3], refs[-3:]
    sums[...] = half_sums(f_own, f_other, w_own, w_other, chunks, halves)
    count = 0
    for chunk in chunks:
        for k in range(chunk.shape[0]):
            heads[count] = chunk[k, : heads.shape[1], :].astype(F32)
            count += 1


def late_kernel(chunk_count, scalars, f_own, f_other, w_own, w_other, hole_weights, *refs):
    chunks, refs = refs[:chunk_count], refs[chunk_count:]
    early, (out, halves, head, hole) = refs[:-4], refs[-4:]
    rows = w_own.shape[1]
    width = f_other.shape[1]
    pairs = hole_weights.shape[0]
    sums = [s[...] for s in early[0::2]]
    sums.append(half_sums(f_own, f_other, w_own, w_other, chunks, halves))
    sums = jnp.concatenate(sums, axis=0)

    local = 0
    for heads in early[1::2]:
        for k in range(heads.shape[0]):
            head[pl.ds(scalars[local], 1)] = heads[k][None]
            local += 1
    for chunk in chunks:
        for k in range(chunk.shape[0]):
            head[pl.ds(scalars[local], 1)] = chunk[k, : head.shape[1], :].astype(F32)[None]
            local += 1
    for a in range(rows):
        hole[:, a, :] = jnp.dot(
            hole_weights[...], head[:, a, :], precision=lax.Precision.HIGHEST,
            preferred_element_type=F32,
        )
    place, chosen = scalars[pairs + 1], scalars[pairs + 2]
    lanes = sums.shape[1]
    for i in range(local):
        term = hole[pl.ds(scalars[i], 1)][0, :rows, :]
        lane = lax.broadcasted_iota(jnp.int32, term.shape, 1)
        mask = (lane >= place) & (lane < place + width) & (chosen == 1)
        both = sums[i * rows : (i + 1) * rows] + jnp.where(mask, term, 0.0)
        both = both[:, : lanes // 2] + both[:, lanes // 2 :]
        both = both + pltpu.roll(both, 64, 1)
        both = both + pltpu.roll(both, 32, 1)
        other = pltpu.roll(both, 16, 1)
        row = lax.broadcasted_iota(jnp.int32, both.shape, 0)
        group = lax.broadcasted_iota(jnp.int32, both.shape, 1) // 16
        for h in range(2):
            tile = jnp.where(row % 2 == h, both, other)
            tile = jnp.sum(jnp.where(group == row, tile, 0.0), axis=0, keepdims=True)
            out[pl.ds(scalars[i] * 2 + h, 1)] = tile[None]


def per_device(amplitudes, factors, hole_weights, driver, eps_vir, pair_energy):
    pairs = hole_weights.shape[0]
    rows, columns = driver.shape[1], driver.shape[2]
    half = factors.shape[2] // 2
    width = factors.shape[1]
    x, ylo, yhi, z, core = (lax.axis_index(name) for name in AXES)
    aux_index = lax.axis_index(AUX)
    pair_index = lax.axis_index(PAIR)
    xs, lows = lax.axis_size("x"), lax.axis_size("ylo")

    own = amplitudes[0]
    split = jnp.stack([own[:, :half], own[:, half:]])
    sent = jnp.tile(split[None], (lax.axis_size("yhi") * lax.axis_size("z"), 1, 1, 1))
    amp = lax.all_to_all(sent.reshape(-1, *split.shape[1:]), AUX, 0, 0, tiled=True)
    amp = amp.reshape(-1, half)

    scattered = window_scattered(factors, rows)
    f_other = lax.dynamic_slice_in_dim(factors, (1 - core) * half, half, 2)
    amp, f_other = lax.optimization_barrier((amp, f_other))
    f_other = swapped(f_other)

    start = (aux_index * columns) % half
    here = lax.dynamic_slice_in_dim(amp[:rows], start, columns, 1)
    there = lax.dynamic_slice_in_dim(amp[:rows], start + columns * (1 - 2 * core), columns, 1)
    amp_cols = jnp.where(core == yhi, here, swapped(there)).astype(F32)

    order = jnp.stack(
        [i * lows + (ylo - k) % lows for k in (0, 1, -1, 2) for i in range(xs)]
    ).astype(jnp.int32)
    place = (pair_index * width) % half
    chosen = (yhi == 0) & (z == 0) & (core == (pair_index * width) // half)
    scalars = jnp.concatenate(
        [order, jnp.stack([core, place, chosen.astype(jnp.int32)]).astype(jnp.int32)]
    )

    spread = window_spread(scattered)
    chunk = collected(amp)
    chunk, amp_cols, scalars = lax.optimization_barrier((chunk, amp_cols, scalars))
    behind, ahead = shifted(chunk, "y", 1), shifted(chunk, "y", -1)
    window = collected(spread)
    window_other = swapped(window)

    head_rows = 8
    blocks = factors.shape[0] // BLOCK_Q
    span = rows * BLOCK_Q
    whole = pl.BlockSpec(memory_space=pltpu.VMEM)
    own_half = pl.BlockSpec((factors.shape[0], width, half), lambda i, s: (0, 0, s[pairs]))
    params = pltpu.CompilerParams(vmem_limit_bytes=44 * 1024 * 1024)

    def scratch(count):
        return pltpu.VMEM((count * span, 2 * blocks * half), BF16)

    def cost(count):
        return pl.CostEstimate(
            flops=1_000_000 * count, bytes_accessed=100_000, transcendentals=0
        )

    def early(*chunks):
        count = sum(c.shape[0] for c in chunks)
        return pl.pallas_call(
            early_kernel,
            grid_spec=pltpu.PrefetchScalarGridSpec(
                num_scalar_prefetch=1,
                grid=(1,),
                in_specs=[own_half] + [whole] * (3 + len(chunks)),
                out_specs=[whole, whole],
                scratch_shapes=[scratch(count)],
            ),
            out_shape=[
                jax.ShapeDtypeStruct((count * rows, BLOCK_Q * width), F32),
                jax.ShapeDtypeStruct((count, head_rows, half), F32),
            ],
            compiler_params=params,
            cost_estimate=cost(count),
        )(scalars, factors, f_other, window, window_other, *chunks)

    cut = xs // 2
    last = (shifted(behind[:cut], "y", 1), shifted(ahead[cut:], "y", -1))
    done = early(chunk, behind, ahead)
    tiles = pl.pallas_call(
        lambda *refs: late_kernel(len(last), *refs),
        grid_spec=pltpu.PrefetchScalarGridSpec(
            num_scalar_prefetch=1,
            grid=(1,),
            in_specs=[own_half] + [whole] * (4 + len(last) + len(done)),
            out_specs=whole,
            scratch_shapes=[
                scratch(lows),
                pltpu.VMEM((pairs, head_rows, half), F32),
                pltpu.VMEM((pairs, head_rows, half), F32),
            ],
        ),
        out_shape=jax.ShapeDtypeStruct((pairs * 2, 1, 128), F32),
        compiler_params=params,
        cost_estimate=cost(lows),
    )(scalars, factors, f_other, window, window_other, hole_weights, *last, *done)

    summed = jnp.sum(lax.all_to_all(tiles, AUX, 0, 0, tiled=True), axis=0)
    count = lax.axis_size(AUX)
    parts = width // columns
    moves = []
    for g in range(pairs):
        for j in range(count):
            moves.append((g * count + j, (j // parts) * count + parts * g + j % parts))
    summed = lax.ppermute(summed, AXES, moves)
    summed = summed[:, : rows * columns].reshape(1, rows, columns)

    residual = driver + summed
    eps_cols = lax.dynamic_slice_in_dim(eps_vir, aux_index * columns, columns, 0)
    denominator = (
        eps_vir[:rows][None, :, None] + eps_cols[None, None, :] - pair_energy[:, None, None]
    )
    new_amps = amp_cols[None] - residual / denominator
    return (residual, new_amps)


def solution(mesh):
    finer = Mesh(mesh.devices.reshape(4, 4, 2, 8, 2), AXES)
    in_specs = (P(PAIR, AUX, None), P(AUX, PAIR, None), P(), P(PAIR, None, AUX), P(), P(PAIR))
    out_specs = (P(PAIR, None, AUX), P(PAIR, None, AUX))
    return jax.shard_map(
        per_device, mesh=finer, in_specs=in_specs, out_specs=out_specs, check_vma=False
    )
```
